128 devices in a mesh: row: 8 (over z_hi, y), col: 16 (over x, z_lo, core).
Axes of the slice: x: 4, y: 4, z: 4 (z_hi: 2, z_lo: 2; z = z_hi * 2 + z_lo), core: 2. Of those that a mesh axis runs over, the one named last changes fastest.
Arguments:
- sim: bfloat16 [16384, 16384], P('row', 'col'), may hold values from -6 to 6
- diag_blocks: bfloat16 [2048, 16384], P(None, 'col'), may hold values from -0.125 to 0.125
- match_perm: int32 [8, 2048], replicated, may hold values from 0 to 2047, each once within a row
- match_scale: float32 [8, 2048], replicated, may hold values from 0.3 to 1.5
- features: bfloat16 [16384, 256], P('col'), may hold values from -0.046875 to 0.046875
Outputs:
- new_sim: bfloat16 [16384, 16384], P('row', 'col')
- aggregated: float32 [16384, 256], P(('row', 'col'))
The draws below stay inside these ranges and needn't reach their ends.
Inputs may be any that keep to these rules, and one draw needn't show every extreme that they name: Each row of match_perm lists every number of 0 to 2047 once.
All inputs are finite; a program needn't handle non-finite values.
Results may differ from the reference program's by a relative error of at most 0.0058.
Values may be sent and summed in bfloat16 or wider, within the bound.
A program may use at most 128 MiB of HBM per device.

```python
import math
import jax
import jax.numpy as jnp
from jax import lax

NB = 2048
F = 256
K = 8
N = 16384
N_COL = 16


def steps_of(own_key, shape, shards, smallest, top_value):
    level, own = 1.0, jax.random.fold_in(own_key, 6)
    for dim, blocks in shards:
        steps = jnp.exp(jax.random.uniform(jax.random.fold_in(own, dim), (blocks,), jnp.float32, smallest / len(shards), top_value / len(shards)))
        level = level * jnp.repeat(steps, shape[dim] // blocks).reshape([-1 if axis == dim else 1 for axis in range(len(shape))])
    return level


def scatter_about(key, extent, deviation, limit, shards=(), kind=jnp.bfloat16):
    result = deviation * jax.random.normal(key, extent, jnp.float32)
    if shards:
        result = result * steps_of(key, extent, shards, -0.22, 0.18)
    return jnp.clip(result, -limit, limit).astype(kind)


def setup_inputs(seed: int = 0) -> dict:
    seeds = jax.random.split(jax.random.key(seed), 6)
    sim = scatter_about(seeds[0], (N, N), 1.0, 6.0, ((0, 8), (1, 16)))
    diag_blocks = scatter_about(seeds[1], (NB, N), NB ** -0.5, 0.125, ((1, 16),))
    match_perm = jax.vmap(lambda own: jax.random.permutation(own, NB))(jax.random.split(seeds[2], K)).reshape((K, NB)).astype(jnp.int32)
    match_scale = jnp.clip(jnp.exp(jax.random.uniform(seeds[3], (K, NB), jnp.float32, math.log(0.3), math.log(1.5))), 0.3, 1.5)
    features = scatter_about(seeds[4], (N, F), N ** -0.5, 0.046875, ((0, 16),))
    return {"sim": sim, "diag_blocks": diag_blocks, "match_perm": match_perm, "match_scale": match_scale, "features": features}


decay_factor = 0.8


def reference(sim, diag_blocks, match_perm, match_scale, features):
    blocks = N_COL // 2
    halfway = blocks // 2
    total = NB * blocks
    columns = []
    for target in range(blocks):
        source = (target + halfway) % blocks
        own_part = sim[:, target * NB:(target + 1) * NB]
        far_part = sim[:, source * NB:(source + 1) * NB]
        moved = (jnp.take(far_part, match_perm[source], axis=1) * match_scale[source][None, :]).astype(jnp.bfloat16)
        product = jnp.dot(own_part, diag_blocks[:, target * NB:(target + 1) * NB], preferred_element_type=jnp.float32)
        columns.append((product + moved).astype(jnp.bfloat16))
    mixed = jnp.concatenate(columns, axis=1)
    row_blocks = []
    for target in range(blocks):
        source = (target + halfway) % blocks
        own_rows = mixed[target * NB:(target + 1) * NB]
        far_rows = mixed[source * NB:(source + 1) * NB]
        moved = (jnp.take(far_rows, match_perm[source], axis=0) * match_scale[source][:, None]).astype(jnp.bfloat16)
        product = lax.dot_general(diag_blocks[:, target * NB:(target + 1) * NB], own_rows, (((0,), (0,)), ((), ())), preferred_element_type=jnp.float32)
        row_blocks.append((decay_factor * (product + moved)).astype(jnp.bfloat16))
    new_sim = jnp.concatenate(row_blocks, axis=0)
    index = jnp.arange(total)
    new_sim = new_sim.at[index, index].set(jnp.ones((total,), new_sim.dtype))
    aggregated = jnp.dot(new_sim, features, preferred_element_type=jnp.float32)
    return new_sim, aggregated
```

```python
import jax
import jax.numpy as jnp
from jax import lax
from jax.experimental import pallas as pl
from jax.experimental.pallas import tpu as pltpu
from jax.sharding import PartitionSpec as P

decay_factor = 0.8
MESH = pl.DeviceIdType.MESH

NB = 2048
HALF = 1024
F = 256
CH = 256
NCH = NB // CH
PIECE = 128
BF16 = jnp.bfloat16
F32 = jnp.float32


def kernel(
    sim, diag, perm, scale, feat,
    new_sim, agg,
    s_own, s_par, b_own, onehot, mixed, sent, marr, bt, acc, feats,
    mine_t, perm_row, scale_row, perm_col, inv_scale, part, slots, total,
    load_sem, own_sem,
    sx, rx, sz, rz, sd, rd, sf, rf, sb, rb, se, sc, rc, sa, ra, out_sem, agg_sem,
):
    row = lax.axis_index("row")
    col = lax.axis_index("col")
    zh, y = row // 4, row % 4
    x, zl, core = col // 4, (col // 2) % 2, col % 2
    block = col // 2
    sibling = (row, col + 1 - 2 * core)
    x_partner = (row, (col + 8) % 16)
    z_partner = ((row + 4) % 8, col)
    near = (row, col + 2 - 4 * zl)
    hold_same = (x // 2 == zh).astype(jnp.int32)
    hold_piece = y + 4 * (1 - hold_same)
    hold_zl = lax.rem(zl + 1 - hold_same, 2)
    parity = y % 2
    match = (parity == zl).astype(jnp.int32)
    first = 4 * (1 - match)
    source_zh = lax.rem(zh + 1 - match, 2)

    def hold_target(i):
        return block, i * 4 + hold_zl * 2 + core

    def hold_source(i):
        return source_zh * 4 + i, (row // 2) * 4 + parity * 2 + core

    def is_me(device):
        return jnp.logical_and(device[0] == row, device[1] == col)

    barrier = pltpu.get_barrier_semaphore()

    def greet(device):
        pl.semaphore_signal(barrier, inc=1, device_id=device, device_id_type=MESH)

    for i in range(1, 16):
        greet((row, (col + i) % 16))
    greet(z_partner)
    own_source = jnp.int32(0)
    for i in range(4):
        device = hold_source(i)

        @pl.when(jnp.logical_not(is_me(device)))
        def _():
            greet(device)

    out_count = jnp.int32(16)
    for i in range(4):
        out_count = out_count + jnp.where(is_me(hold_target(i)), 0, 1)

    loads = [
        pltpu.make_async_copy(diag, b_own, load_sem.at[0]),
        pltpu.make_async_copy(feat, feats, load_sem.at[1]),
    ]
    for load in loads:
        load.start()

    def own_load(i):
        rows = pl.ds(i * CH, CH)
        return pltpu.make_async_copy(
            sim.at[rows], s_own.at[core, rows], own_sem.at[i]
        )

    for i in range(NCH):
        own_load(i).start()
    pl.semaphore_wait(barrier, out_count)

    def remote(src, dst, send, recv, device):
        return pltpu.make_async_remote_copy(
            src_ref=src, dst_ref=dst, send_sem=send, recv_sem=recv,
            device_id=device, device_id_type=MESH,
        )

    def x_copy(i):
        rows = pl.ds(i * CH, CH)
        return remote(sim.at[rows], s_par.at[core, rows], sx.at[i], rx.at[i], x_partner)

    def own_copy(i):
        rows = pl.ds(i * CH, CH)
        return remote(sim.at[rows], s_own.at[core, rows], sd.at[i], rd.at[i], sibling)

    def own_arrival(i):
        rows = pl.ds(i * CH, CH)
        return remote(sim.at[rows], s_own.at[1 - core, rows], sd.at[i], rd.at[i], sibling)

    def forward(i):
        rows = pl.ds(i * CH, CH)
        return remote(s_par.at[core, rows], s_par.at[core, rows], sf.at[i], rf.at[i], sibling)

    def forward_arrival(i):
        rows = pl.ds(i * CH, CH)
        return remote(s_par.at[core, rows], s_par.at[1 - core, rows], sf.at[i], rf.at[i], sibling)

    def z_copy(i):
        rows = pl.ds(i * CH, CH)
        return remote(sent.at[rows], marr.at[rows], sz.at[i], rz.at[i], z_partner)

    def bt_rows(half, piece):
        return pl.ds(pl.multiple_of(half * HALF + piece * PIECE, PIECE), PIECE)

    def piece_copy(i):
        device = hold_target(i)
        return remote(
            mine_t, bt.at[bt_rows(core, hold_piece)], sb.at[i], rb.at[hold_piece], device
        )

    def piece_arrival(q):
        return remote(mine_t, bt.at[bt_rows(core, q)], sb.at[0], rb.at[q], near)

    def near_copy(i):
        rows = bt_rows(core, first + i)
        return remote(bt.at[rows], bt.at[rows], se.at[i], rb.at[first + i], near)

    def core_copy(q):
        rows = bt_rows(core, q)
        return remote(bt.at[rows], bt.at[rows], sc.at[q], rc.at[q], sibling)

    def core_arrival(q):
        return remote(mine_t, bt.at[bt_rows(1 - core, q)], sc.at[q], rc.at[q], sibling)

    for i in range(2):
        x_copy(i).start()
    for i in range(NCH):
        own_copy(i).start()

    loads[0].wait()
    piece_cols = pl.ds(pl.multiple_of(hold_piece * PIECE, PIECE), PIECE)
    for i in range(NB // PIECE):
        rows = pl.ds(i * PIECE, PIECE)
        mine_t[:, rows] = b_own[rows, piece_cols].astype(F32).T.astype(BF16)
    for i in range(4):
        device = hold_target(i)
        self_copy = is_me(device)

        @pl.when(jnp.logical_not(self_copy))
        def _():
            piece_copy(i).start()

        @pl.when(self_copy)
        def _():
            pltpu.make_async_copy(
                mine_t, bt.at[bt_rows(core, hold_piece)], rb.at[hold_piece]
            ).start()

    col_source = (block + 4) % 8
    row_source = (row + 4) % 8
    lines = lax.broadcasted_iota(jnp.int32, (8, NB), 0)

    def line(table, wanted):
        return jnp.sum(jnp.where(lines == wanted, table[...], 0), axis=0, keepdims=True)

    perm_row[0:1, :] = line(perm, col_source)
    perm_row[1:2, :] = line(perm, row_source)
    perm_row[2:3, :] = line(perm, row)
    scale_row[0:1, :] = line(scale, col_source)
    scale_row[1:2, :] = line(scale, row)

    half_cols = pl.ds(pl.multiple_of(core * HALF, HALF), HALF)

    @pl.loop(0, NB // 128)
    def _(i):
        rows = pl.ds(i * 128, 128)
        wanted = perm_row[0:1, half_cols]
        here = lax.broadcasted_iota(jnp.int32, (128, HALF), 0) + i * 128
        onehot[rows, :] = jnp.where(here == wanted, 1.0, 0.0).astype(BF16)

    for i in range(NB // 128):
        part_row = perm_row[1:2, pl.ds(i * 128, 128)]
        perm_col[pl.ds(i * 128, 128), :] = jnp.broadcast_to(part_row, (128, 128)).T

    @pl.loop(0, NB // 128)
    def _(i):
        rows = pl.ds(i * 128, 128)
        here = lax.broadcasted_iota(jnp.int32, (128, NB), 0) + i * 128
        hit = jnp.where(here == perm_row[2:3, :], scale_row[1:2, :], 0.0)
        inv_scale[rows, :] = jnp.broadcast_to(jnp.sum(hit, axis=1, keepdims=True), (128, 128))

    @pl.loop(0, NCH)
    def _(i):
        rows = pl.ds(pl.multiple_of(i * CH, CH), CH)

        @pl.when(i + 2 < NCH)
        def _():
            x_copy(i + 2).start()

        x_copy(i).wait_recv()
        forward(i).start()

        @pl.when(jnp.logical_and(i >= 2, i < 6))
        def _():
            piece_arrival(first + i - 2).wait_recv()
            near_copy(i - 2).start()
            core_copy(first + i - 2).start()

        own_load(i).wait()
        own_arrival(i).wait_recv()
        forward_arrival(i).wait_recv()

        @pl.loop(0, HALF // 256)
        def _(n):
            cols = pl.ds(pl.multiple_of(n * 256, 256), 256)
            value = jnp.dot(s_own[0, rows, :], b_own[:HALF, cols], preferred_element_type=F32)
            value += jnp.dot(s_own[1, rows, :], b_own[HALF:, cols], preferred_element_type=F32)
            moved = jnp.dot(s_par[0, rows, :], onehot[:HALF, cols], preferred_element_type=F32)
            moved += jnp.dot(s_par[1, rows, :], onehot[HALF:, cols], preferred_element_type=F32)
            here = pl.ds(pl.multiple_of(core * HALF + n * 256, 256), 256)
            value += moved * scale_row[0:1, here]
            value = value.astype(BF16)
            mixed[rows, cols] = value
            lanes = inv_scale[rows, :]
            sent[rows, cols] = (
                value.astype(F32) * jnp.concatenate([lanes, lanes], axis=1)
            ).astype(BF16)

        z_copy(i).start()

    other = 4 - first

    @pl.loop(0, 4)
    def _(i):
        piece_arrival(other + i).wait_recv()
        core_copy(other + i).start()

    @pl.loop(0, 8)
    def _(q):
        core_arrival(q).wait_recv()

    @pl.loop(0, NCH)
    def _(t):
        rows = pl.ds(pl.multiple_of(t * CH, CH), CH)

        @pl.loop(0, HALF // 512)
        def _(n):
            cols = pl.ds(pl.multiple_of(n * 512, 512), 512)
            acc[rows, cols] = jnp.dot(bt[rows, :], mixed[:, cols], preferred_element_type=F32)

    def gathered(rows, i, cols):
        wanted = perm_col[rows, :]
        wanted = jnp.concatenate([wanted, wanted], axis=1)
        here = lax.broadcasted_iota(jnp.int32, (CH, CH), 1) + i * CH
        pick = jnp.where(here == wanted, 1.0, 0.0).astype(BF16)
        far = marr[pl.ds(pl.multiple_of(i * CH, CH), CH), cols]
        return jnp.dot(pick, far, preferred_element_type=F32)

    @pl.loop(0, NCH - 1)
    def _(i):
        z_copy(i).wait_recv()

        @pl.loop(0, NCH)
        def _(t):
            rows = pl.ds(pl.multiple_of(t * CH, CH), CH)
            acc[rows, :] += gathered(rows, i, pl.ds(0, HALF))

    z_copy(NCH - 1).wait_recv()
    loads[1].wait()
    offset = col * HALF - row * NB

    def out_copy(t):
        rows = pl.ds(pl.multiple_of(t * CH, CH), CH)
        return pltpu.make_async_copy(mixed.at[rows], new_sim.at[rows], out_sem.at[t])

    def part_copy(owner):
        rows = pl.ds(pl.multiple_of(owner * 128, 128), 128)
        return remote(part.at[rows], slots.at[col], sa.at[owner], ra.at[col], (row, owner))

    def part_arrival(i):
        return remote(part.at[pl.ds(0, 128)], slots.at[i], sa.at[i], ra.at[i], sibling)

    @pl.loop(0, NCH)
    def _(t):
        rows = pl.ds(pl.multiple_of(t * CH, CH), CH)
        value = decay_factor * (acc[rows, :] + gathered(rows, NCH - 1, pl.ds(0, HALF)))
        down = lax.broadcasted_iota(jnp.int32, (CH, HALF), 0) + t * CH
        across = lax.broadcasted_iota(jnp.int32, (CH, HALF), 1) + offset
        value = jnp.where(down == across, 1.0, value).astype(BF16)
        mixed[rows, :] = value
        out_copy(t).start()
        part[rows, :] = jnp.dot(value, feats[...], preferred_element_type=F32).astype(BF16)
        for k in range(2):
            owner = 2 * t + k

            @pl.when(owner != col)
            def _():
                part_copy(owner).start()

    mine = part[pl.ds(pl.multiple_of(col * 128, 128), 128), :].astype(F32)
    total[...] = mine

    @pl.loop(0, 16)
    def _(i):
        @pl.when(i != col)
        def _():
            part_arrival(i).wait_recv()
            total[...] += slots[i].astype(F32)

    agg_copy = pltpu.make_async_copy(total, agg, agg_sem)
    agg_copy.start()

    @pl.loop(0, NCH)
    def _(i):
        x_copy(i).wait_send()
        own_copy(i).wait_send()
        forward(i).wait_send()
        z_copy(i).wait_send()
        core_copy(i).wait_send()
        out_copy(i).wait()

    for i in range(4):
        near_copy(i).wait_send()

        @pl.when(jnp.logical_not(is_me(hold_target(i))))
        def _():
            piece_copy(i).wait_send()

    @pl.loop(0, 16)
    def _(i):
        @pl.when(i != col)
        def _():
            part_copy(i).wait_send()

    agg_copy.wait()


def on_device(sim, diag_blocks, match_perm, match_scale, features):
    dma = pltpu.SemaphoreType.DMA
    return pl.pallas_call(
        kernel,
        out_shape=(
            jax.ShapeDtypeStruct((NB, HALF), BF16),
            jax.ShapeDtypeStruct((128, F), F32),
        ),
        in_specs=[
            pl.BlockSpec(memory_space=pl.ANY),
            pl.BlockSpec(memory_space=pl.ANY),
            pl.BlockSpec(memory_space=pltpu.VMEM),
            pl.BlockSpec(memory_space=pltpu.VMEM),
            pl.BlockSpec(memory_space=pl.ANY),
        ],
        out_specs=(
            pl.BlockSpec(memory_space=pl.ANY),
            pl.BlockSpec(memory_space=pl.ANY),
        ),
        scratch_shapes=[
            pltpu.VMEM((2, NB, HALF), BF16),
            pltpu.VMEM((2, NB, HALF), BF16),
            pltpu.VMEM((NB, HALF), BF16),
            pltpu.VMEM((NB, HALF), BF16),
            pltpu.VMEM((NB, HALF), BF16),
            pltpu.VMEM((NB, HALF), BF16),
            pltpu.VMEM((NB, HALF), BF16),
            pltpu.VMEM((NB, NB), BF16),
            pltpu.VMEM((NB, HALF), F32),
            pltpu.VMEM((HALF, F), BF16),
            pltpu.VMEM((PIECE, NB), BF16),
            pltpu.VMEM((8, NB), jnp.int32),
            pltpu.VMEM((8, NB), F32),
            pltpu.VMEM((NB, 128), jnp.int32),
            pltpu.VMEM((NB, 128), F32),
            pltpu.VMEM((NB, F), BF16),
            pltpu.VMEM((16, 128, F), BF16),
            pltpu.VMEM((128, F), F32),
            dma((2,)), dma((NCH,)),
            dma((NCH,)), dma((NCH,)),
            dma((NCH,)), dma((NCH,)),
            dma((NCH,)), dma((NCH,)),
            dma((NCH,)), dma((NCH,)),
            dma((4,)), dma((8,)), dma((4,)),
            dma((8,)), dma((8,)),
            dma((16,)), dma((16,)),
            dma((NCH,)), dma(()),
        ],
        compiler_params=pltpu.CompilerParams(
            collective_id=0, has_side_effects=True, vmem_limit_bytes=60 * 2**20
        ),
        name="simrank",
    )(sim, diag_blocks, match_perm, match_scale, features)


def solution(mesh):
    placed = (P("row", "col"), P(None, "col"), P(), P(), P("col", None))
    return jax.shard_map(
        on_device,
        mesh=mesh,
        in_specs=placed,
        out_specs=(P("row", "col"), P(("row", "col"), None)),
        check_vma=False,
    )
```

```python
import jax
import jax.numpy as jnp
from jax import lax
from jax.experimental import pallas as pl
from jax.experimental.pallas import tpu as pltpu
from jax.sharding import PartitionSpec as P

decay_factor = 0.8
MESH = pl.DeviceIdType.MESH

NB = 2048
HALF = 1024
F = 256
CH = 256
NCH = NB // CH
PIECE = 256
NSUB = 4
SUB = PIECE // NSUB
AHEAD = 3
LAG = 2
HOME_AT = (0, 1)
PASS_AT = ((), (), (0, 1), (2, 3), (4, 5), (6, 7), (), ())
TAKE_AT = ((), (), (), (0, 1), (2, 3), (4, 5), (6, 7), ())
AFTER_PASS = ((), ())
AFTER_TAKE = ((), ())
AFTER_CROSS = (tuple(range(16)), ())
BF16 = jnp.bfloat16
F32 = jnp.float32


def kernel(
    sim, diag, perm, scale, feat,
    new_sim, agg, relay,
    s_own, s_par, b_own, onehot, mixed, sent, marr, bt, acc, feats,
    mine_t, perm_row, scale_row, perm_col, inv_scale, part, slots, total,
    load_sem, own_sem,
    sx, rx, sz, rz, sd, rd, sf, rf, sb, rb, sq, rq, sy, ry, sc, rc, sa, ra, out_sem, agg_sem,
):
    row = lax.axis_index("row")
    col = lax.axis_index("col")
    zh, y = row // 4, row % 4
    x, zl, core = col // 4, (col // 2) % 2, col % 2
    block = col // 2
    sibling = (row, col + 1 - 2 * core)
    x_partner = (row, (col + 8) % 16)
    z_partner = ((row + 4) % 8, col)
    z_near = (row, col + 2 - 4 * zl)
    z_mirror = ((1 - zh) * 4 + y, x * 4 + (1 - zl) * 2 + core)
    x_pair = (row, col + 4 - 8 * (x % 2))
    x_other = (row, (col + 12 + 8 * (x % 2)) % 16)
    home = x // 2 == zh
    home_int = home.astype(jnp.int32)
    pair = 2 * lax.rem(x + 1 - home_int, 2)
    order = (pair + zl, pair + 1 - zl, 2 - pair + zl, 3 - pair - zl)
    held = 2 * (x % 2) + zl

    barrier = pltpu.get_barrier_semaphore()

    def greet(device):
        pl.semaphore_signal(barrier, inc=1, device_id=device, device_id_type=MESH)

    for i in range(1, 16):
        greet((row, (col + i) % 16))
    for i in range(1, 4):
        greet((zh * 4 + (y + i) % 4, col))
    greet(z_partner)
    greet(z_mirror)

    loads = [
        pltpu.make_async_copy(diag, b_own, load_sem.at[0]),
        pltpu.make_async_copy(feat, feats, load_sem.at[1]),
    ]
    for load in loads:
        load.start()

    def own_load(i):
        rows = pl.ds(i * CH, CH)
        return pltpu.make_async_copy(
            sim.at[rows], s_own.at[core, rows], own_sem.at[i]
        )

    for i in range(NCH):
        own_load(i).start()
    pl.semaphore_wait(barrier, 20)

    def remote(src, dst, send, recv, device):
        return pltpu.make_async_remote_copy(
            src_ref=src, dst_ref=dst, send_sem=send, recv_sem=recv,
            device_id=device, device_id_type=MESH,
        )

    def x_copy(i):
        rows = pl.ds(i * CH, CH)
        return remote(sim.at[rows], s_par.at[core, rows], sx.at[i], rx.at[i], x_partner)

    def own_copy(i):
        rows = pl.ds(i * CH, CH)
        return remote(sim.at[rows], s_own.at[core, rows], sd.at[i], rd.at[i], sibling)

    def own_arrival(i):
        rows = pl.ds(i * CH, CH)
        return remote(sim.at[rows], s_own.at[1 - core, rows], sd.at[i], rd.at[i], sibling)

    def forward(i):
        rows = pl.ds(i * CH, CH)
        return remote(s_par.at[core, rows], s_par.at[core, rows], sf.at[i], rf.at[i], sibling)

    def forward_arrival(i):
        rows = pl.ds(i * CH, CH)
        return remote(s_par.at[core, rows], s_par.at[1 - core, rows], sf.at[i], rf.at[i], sibling)

    def z_copy(i):
        rows = pl.ds(i * CH, CH)
        return remote(sent.at[rows], marr.at[rows], sz.at[i], rz.at[i], z_partner)

    def bt_rows(half, part_of):
        return bt.at[pl.ds(pl.multiple_of(half * HALF + part_of * PIECE, PIECE), PIECE)]

    def near_half():
        rows = pl.ds(0, PIECE // 2)
        return remote(
            mine_t.at[rows], relay.at[held, rows], sb.at[0], rb.at[0], z_near
        )

    def mirror_half():
        rows = pl.ds(PIECE // 2, PIECE // 2)
        return remote(
            mine_t.at[rows], relay.at[held, rows], sb.at[1], rb.at[1], z_mirror
        )

    def held_copy(n):
        rows = pl.ds(n * SUB, SUB)
        return pltpu.make_async_copy(mine_t.at[rows], relay.at[held, rows], rq.at[held, n])

    def sub(n):
        return pl.ds(n * SUB, SUB)

    def along_x(k, n, where):
        device = (x_pair, x_other)[where]
        source = order[k]
        return remote(
            relay.at[source, sub(n)], relay.at[source, sub(n)],
            sq.at[k % 2, where, n], rq.at[source, n], device,
        )

    def bt_sub(half, u, n):
        start = pl.multiple_of(half * HALF + u * PIECE + n * SUB, SUB)
        return bt.at[pl.ds(start, SUB)]

    def along_y(target, n):
        return remote(
            relay.at[target, sub(n)], bt_sub(core, y, n),
            sy.at[target, n], ry.at[y, n], (zh * 4 + target, col),
        )

    def stay(n):
        return pltpu.make_async_copy(relay.at[y, sub(n)], bt_sub(core, y, n), ry.at[y, n])

    def y_arrival(u, n):
        return remote(mine_t.at[sub(n)], bt_sub(core, u, n), sy.at[u, n], ry.at[u, n], sibling)

    def core_copy(u, n):
        return remote(
            bt_sub(core, u, n), bt_sub(core, u, n), sc.at[u, n], rc.at[u, n], sibling
        )

    def core_arrival(u, n):
        return remote(
            mine_t.at[sub(n)], bt_sub(1 - core, u, n), sc.at[u, n], rc.at[u, n], sibling
        )

    def give_y(target, n):
        @pl.when(target != y)
        def _():
            along_y(target, n).start()

        @pl.when(target == y)
        def _():
            stay(n).start()

    def hand_out(k):
        for n in range(NSUB):
            along_x(k, n, 0).start()
            along_x(k, n, 1).start()
        for n in range(NSUB):
            give_y(order[k], n)

    def pass_on(m):
        k, n = m // NSUB, m % NSUB

        @pl.when(jnp.logical_not(home))
        def _():
            along_x(k, n, 0).wait_recv()
            along_x(k, n, 0).start()
            give_y(order[k], n)

    def take_in(m):
        k, n = 2 + m // NSUB, m % NSUB
        along_x(k, n, 0).wait_recv()
        give_y(order[k], n)

    def cross(m):
        u, n = m // NSUB, m % NSUB
        y_arrival(u, n).wait_recv()
        core_copy(u, n).start()

    for i in range(AHEAD):
        x_copy(i).start()
    for i in range(NCH):
        own_copy(i).start()

    loads[0].wait()
    piece_cols = pl.ds(pl.multiple_of(y * PIECE, PIECE), PIECE)
    for i in range(NB // PIECE):
        rows = pl.ds(i * PIECE, PIECE)
        mine_t[:, rows] = b_own[rows, piece_cols].astype(F32).T.astype(BF16)

    @pl.when(home)
    def _():
        near_half().start()
        for n in range(NSUB):
            held_copy(n).start()

    @pl.when(jnp.logical_not(home))
    def _():
        mirror_half().start()

    col_source = (block + 4) % 8
    row_source = (row + 4) % 8
    lines = lax.broadcasted_iota(jnp.int32, (8, NB), 0)

    def line(table, wanted):
        return jnp.sum(jnp.where(lines == wanted, table[...], 0), axis=0, keepdims=True)

    perm_row[0:1, :] = line(perm, col_source)
    perm_row[1:2, :] = line(perm, row_source)
    perm_row[2:3, :] = line(perm, row)
    scale_row[0:1, :] = line(scale, col_source)
    scale_row[1:2, :] = line(scale, row)

    half_cols = pl.ds(pl.multiple_of(core * HALF, HALF), HALF)

    @pl.loop(0, NB // 128)
    def _(i):
        rows = pl.ds(i * 128, 128)
        wanted = perm_row[0:1, half_cols]
        here = lax.broadcasted_iota(jnp.int32, (128, HALF), 0) + i * 128
        onehot[rows, :] = jnp.where(here == wanted, 1.0, 0.0).astype(BF16)

    for i in range(NB // 128):
        part_row = perm_row[1:2, pl.ds(i * 128, 128)]
        perm_col[pl.ds(i * 128, 128), :] = jnp.broadcast_to(part_row, (128, 128)).T

    @pl.loop(0, NB // 128)
    def _(i):
        rows = pl.ds(i * 128, 128)
        here = lax.broadcasted_iota(jnp.int32, (128, NB), 0) + i * 128
        hit = jnp.where(here == perm_row[2:3, :], scale_row[1:2, :], 0.0)
        inv_scale[rows, :] = jnp.broadcast_to(jnp.sum(hit, axis=1, keepdims=True), (128, 128))

    def gathered(rows, i):
        wanted = perm_col[rows, :]
        wanted = jnp.concatenate([wanted, wanted], axis=1)
        here = lax.broadcasted_iota(jnp.int32, (CH, CH), 1) + i * CH
        pick = jnp.where(here == wanted, 1.0, 0.0).astype(BF16)
        far = marr[pl.ds(pl.multiple_of(i * CH, CH), CH), :]
        return jnp.dot(pick, far, preferred_element_type=F32)

    def add_matched(i):
        z_copy(i).wait_recv()

        @pl.loop(0, NCH)
        def _(t):
            rows = pl.ds(pl.multiple_of(t * CH, CH), CH)
            far = gathered(rows, i)

            @pl.when(i == 0)
            def _():
                acc[rows, :] = far

            @pl.when(i > 0)
            def _():
                acc[rows, :] += far

    @pl.loop(0, NCH)
    def _(i):
        rows = pl.ds(pl.multiple_of(i * CH, CH), CH)

        @pl.when(i + AHEAD < NCH)
        def _():
            x_copy(i + AHEAD).start()

        x_copy(i).wait_recv()
        forward(i).start()

        own_load(i).wait()
        own_arrival(i).wait_recv()
        forward_arrival(i).wait_recv()

        @pl.loop(0, HALF // 256)
        def _(n):
            cols = pl.ds(pl.multiple_of(n * 256, 256), 256)
            value = jnp.dot(s_own[0, rows, :], b_own[:HALF, cols], preferred_element_type=F32)
            value += jnp.dot(s_own[1, rows, :], b_own[HALF:, cols], preferred_element_type=F32)
            moved = jnp.dot(s_par[0, rows, :], onehot[:HALF, cols], preferred_element_type=F32)
            moved += jnp.dot(s_par[1, rows, :], onehot[HALF:, cols], preferred_element_type=F32)
            here = pl.ds(pl.multiple_of(core * HALF + n * 256, 256), 256)
            value += moved * scale_row[0:1, here]
            value = value.astype(BF16)
            mixed[rows, cols] = value
            lanes = inv_scale[rows, :]
            sent[rows, cols] = (
                value.astype(F32) * jnp.concatenate([lanes, lanes], axis=1)
            ).astype(BF16)

        z_copy(i).start()

        @pl.when(jnp.logical_and(home, i == HOME_AT[0]))
        def _():
            for n in range(NSUB):
                held_copy(n).wait()
            hand_out(0)

        @pl.when(jnp.logical_and(home, i == HOME_AT[1]))
        def _():
            near_half().wait_recv()
            mirror_half().wait_recv()
            hand_out(1)

        for step in range(NCH):
            if PASS_AT[step] or TAKE_AT[step]:
                @pl.when(i == step)
                def _():
                    for m in PASS_AT[step]:
                        pass_on(m)
                    for m in TAKE_AT[step]:
                        take_in(m)

        @pl.when(i >= LAG)
        def _():
            add_matched(i - LAG)

    for i in range(NCH - LAG, NCH):
        for m in AFTER_PASS[i - NCH + LAG]:
            pass_on(m)
        for m in AFTER_TAKE[i - NCH + LAG]:
            take_in(m)
        for m in AFTER_CROSS[i - NCH + LAG]:
            cross(m)
        add_matched(i)

    loads[1].wait()
    offset = col * HALF - row * NB

    def out_copy(t):
        rows = pl.ds(pl.multiple_of(t * CH, CH), CH)
        return pltpu.make_async_copy(sent.at[rows], new_sim.at[rows], out_sem.at[t])

    def part_copy(owner):
        rows = pl.ds(pl.multiple_of(owner * 128, 128), 128)
        return remote(part.at[rows], slots.at[col], sa.at[owner], ra.at[col], (row, owner))

    def part_arrival(i):
        return remote(part.at[pl.ds(0, 128)], slots.at[i], sa.at[i], ra.at[i], sibling)

    @pl.loop(0, NCH)
    def _(i):
        z_copy(i).wait_send()

    @pl.loop(0, NCH)
    def _(step):
        u = step // 2
        half = lax.rem(step + core, 2)
        t = half * (NCH // 2) + u
        rows = pl.ds(pl.multiple_of(t * CH, CH), CH)

        @pl.when(half != core)
        def _():
            for n in range(NSUB):
                core_arrival(u, n).wait_recv()

        value = acc[rows, :] + jnp.dot(bt[rows, :], mixed[...], preferred_element_type=F32)
        value = decay_factor * value
        down = lax.broadcasted_iota(jnp.int32, (CH, HALF), 0) + t * CH
        across = lax.broadcasted_iota(jnp.int32, (CH, HALF), 1) + offset
        value = jnp.where(down == across, 1.0, value).astype(BF16)
        sent[rows, :] = value
        out_copy(t).start()
        part[rows, :] = jnp.dot(value, feats[...], preferred_element_type=F32).astype(BF16)
        for k in range(2):
            owner = 2 * t + k

            @pl.when(owner != col)
            def _():
                part_copy(owner).start()

    mine = part[pl.ds(pl.multiple_of(col * 128, 128), 128), :].astype(F32)
    total[...] = mine

    @pl.loop(0, 16)
    def _(i):
        @pl.when(i != col)
        def _():
            part_arrival(i).wait_recv()
            total[...] += slots[i].astype(F32)

    agg_copy = pltpu.make_async_copy(total, agg, agg_sem)
    agg_copy.start()

    @pl.loop(0, NCH)
    def _(i):
        x_copy(i).wait_send()
        own_copy(i).wait_send()
        forward(i).wait_send()
        out_copy(i).wait()

    for n in range(NSUB):
        for u in range(4):
            core_copy(u, n).wait_send()

            @pl.when(u != y)
            def _():
                along_y(u, n).wait_send()

        for k in range(2):
            along_x(k, n, 0).wait_send()

            @pl.when(home)
            def _():
                along_x(k, n, 1).wait_send()

    @pl.when(home)
    def _():
        near_half().wait_send()

    @pl.when(jnp.logical_not(home))
    def _():
        mirror_half().wait_send()

    @pl.loop(0, 16)
    def _(i):
        @pl.when(i != col)
        def _():
            part_copy(i).wait_send()

    agg_copy.wait()


def on_device(sim, diag_blocks, match_perm, match_scale, features):
    dma = pltpu.SemaphoreType.DMA
    return pl.pallas_call(
        kernel,
        out_shape=(
            jax.ShapeDtypeStruct((NB, HALF), BF16),
            jax.ShapeDtypeStruct((128, F), F32),
            jax.ShapeDtypeStruct((4, PIECE, NB), BF16),
        ),
        in_specs=[
            pl.BlockSpec(memory_space=pl.ANY),
            pl.BlockSpec(memory_space=pl.ANY),
            pl.BlockSpec(memory_space=pltpu.VMEM),
            pl.BlockSpec(memory_space=pltpu.VMEM),
            pl.BlockSpec(memory_space=pl.ANY),
        ],
        out_specs=(
            pl.BlockSpec(memory_space=pl.ANY),
            pl.BlockSpec(memory_space=pl.ANY),
            pl.BlockSpec(memory_space=pl.ANY),
        ),
        scratch_shapes=[
            pltpu.VMEM((2, NB, HALF), BF16),
            pltpu.VMEM((2, NB, HALF), BF16),
            pltpu.VMEM((NB, HALF), BF16),
            pltpu.VMEM((NB, HALF), BF16),
            pltpu.VMEM((NB, HALF), BF16),
            pltpu.VMEM((NB, HALF), BF16),
            pltpu.VMEM((NB, HALF), BF16),
            pltpu.VMEM((NB, NB), BF16),
            pltpu.VMEM((NB, HALF), F32),
            pltpu.VMEM((HALF, F), BF16),
            pltpu.VMEM((PIECE, NB), BF16),
            pltpu.VMEM((8, NB), jnp.int32),
            pltpu.VMEM((8, NB), F32),
            pltpu.VMEM((NB, 128), jnp.int32),
            pltpu.VMEM((NB, 128), F32),
            pltpu.VMEM((NB, F), BF16),
            pltpu.VMEM((16, 128, F), BF16),
            pltpu.VMEM((128, F), F32),
            dma((2,)), dma((NCH,)),
            dma((NCH,)), dma((NCH,)),
            dma((NCH,)), dma((NCH,)),
            dma((NCH,)), dma((NCH,)),
            dma((NCH,)), dma((NCH,)),
            dma((2,)), dma((2,)),
            dma((2, 2, NSUB)), dma((4, NSUB)),
            dma((4, NSUB)), dma((4, NSUB)),
            dma((4, NSUB)), dma((4, NSUB)),
            dma((16,)), dma((16,)),
            dma((NCH,)), dma(()),
        ],
        compiler_params=pltpu.CompilerParams(
            collective_id=0, has_side_effects=True, vmem_limit_bytes=60 * 2**20
        ),
        name="simrank",
    )(sim, diag_blocks, match_perm, match_scale, features)[:2]


def solution(mesh):
    placed = (P("row", "col"), P(None, "col"), P(), P(), P("col", None))
    return jax.shard_map(
        on_device,
        mesh=mesh,
        in_specs=placed,
        out_specs=(P("row", "col"), P(("row", "col"), None)),
        check_vma=False,
    )
```

```python
import jax
import jax.numpy as jnp
from jax import lax
from jax.experimental import pallas as pl
from jax.experimental.pallas import tpu as pltpu
from jax.sharding import PartitionSpec as P

decay_factor = 0.8
MESH = pl.DeviceIdType.MESH

NB = 2048
HALF = 1024
F = 256
CH = 256
NCH = NB // CH
PIECE = 256
NSUB = 4
OVER_Z = 2
SUB = PIECE // NSUB
AHEAD = 2
LAG = 2
PASS_AT = ((0, 1), (2, 3), (4, 5), (6, 7), (), (), (), ())
TAKE_AT = ((0,), (1, 2), (3, 4), (5, 6), (7,), (), (), ())
AFTER_PASS = ()
AFTER_TAKE = ()
BF16 = jnp.bfloat16
F32 = jnp.float32


def kernel(
    sim, diag, perm, scale, feat,
    new_sim, agg, relay,
    s_own, s_par, b_own, onehot, mixed, sent, marr, bt, acc, feats,
    mine_t, perm_row, scale_row, perm_col, inv_scale, part, slots, total,
    load_sem, own_sem,
    sx, rx, sz, rz, sd, rd, sf, rf, sb, rb, sq, rq, sv, sy, ry, sc, rc, sp, rp, sa, ra, out_sem, agg_sem,
):
    row = lax.axis_index("row")
    col = lax.axis_index("col")
    zh, y = row // 4, row % 4
    x, zl, core = col // 4, (col // 2) % 2, col % 2
    block = col // 2
    sibling = (row, col + 1 - 2 * core)
    x_partner = (row, (col + 8) % 16)
    z_partner = ((row + 4) % 8, col)
    z_near = (row, col + 2 - 4 * zl)
    z_mirror = ((1 - zh) * 4 + y, x * 4 + (1 - zl) * 2 + core)
    x_pair = (row, col + 4 - 8 * (x % 2))
    x_other = (row, (col + 12 + 8 * (x % 2)) % 16)
    home = x // 2 == zh
    home_int = home.astype(jnp.int32)
    pair = 2 * lax.rem(x + 1 - home_int, 2)
    order = (pair + zl, pair + 1 - zl, 2 - pair + zl, 3 - pair - zl)
    held = 2 * (x % 2) + zl

    barrier = pltpu.get_barrier_semaphore()

    def greet(device):
        pl.semaphore_signal(barrier, inc=1, device_id=device, device_id_type=MESH)

    for i in range(1, 16):
        greet((row, (col + i) % 16))
    for i in range(1, 4):
        greet((zh * 4 + (y + i) % 4, col))
    greet(z_partner)
    greet(z_mirror)

    loads = [
        pltpu.make_async_copy(diag, b_own, load_sem.at[0]),
        pltpu.make_async_copy(feat, feats, load_sem.at[1]),
    ]
    for load in loads:
        load.start()

    def own_load(i):
        rows = pl.ds(i * CH, CH)
        return pltpu.make_async_copy(
            sim.at[rows], s_own.at[core, rows], own_sem.at[i]
        )

    for i in range(NCH):
        own_load(i).start()
    pl.semaphore_wait(barrier, 20)

    def remote(src, dst, send, recv, device):
        return pltpu.make_async_remote_copy(
            src_ref=src, dst_ref=dst, send_sem=send, recv_sem=recv,
            device_id=device, device_id_type=MESH,
        )

    def x_copy(i):
        rows = pl.ds(i * CH, CH)
        return remote(sim.at[rows], s_par.at[core, rows], sx.at[i], rx.at[i], x_partner)

    def own_copy(i):
        rows = pl.ds(i * CH, CH)
        return remote(sim.at[rows], s_own.at[core, rows], sd.at[i], rd.at[i], sibling)

    def own_arrival(i):
        rows = pl.ds(i * CH, CH)
        return remote(sim.at[rows], s_own.at[1 - core, rows], sd.at[i], rd.at[i], sibling)

    def forward(i):
        rows = pl.ds(i * CH, CH)
        return remote(s_par.at[core, rows], s_par.at[core, rows], sf.at[i], rf.at[i], sibling)

    def forward_arrival(i):
        rows = pl.ds(i * CH, CH)
        return remote(s_par.at[core, rows], s_par.at[1 - core, rows], sf.at[i], rf.at[i], sibling)

    def z_copy(i):
        rows = pl.ds(i * CH, CH)
        return remote(sent.at[rows], marr.at[rows], sz.at[i], rz.at[i], z_partner)

    def bt_rows(half, part_of):
        return bt.at[pl.ds(pl.multiple_of(half * HALF + part_of * PIECE, PIECE), PIECE)]

    def near_half():
        rows = pl.ds(0, PIECE // 2)
        return remote(
            mine_t.at[rows], relay.at[held, rows], sb.at[0], rb.at[0], z_near
        )

    def mirror_half():
        rows = pl.ds(PIECE // 2, PIECE // 2)
        return remote(
            mine_t.at[rows], relay.at[held, rows], sb.at[1], rb.at[1], z_mirror
        )

    def held_copy(n):
        rows = pl.ds(n * SUB, SUB)
        return pltpu.make_async_copy(mine_t.at[rows], relay.at[held, rows], rq.at[held, n])

    def sub(n):
        return pl.ds(n * SUB, SUB)

    def along_x(k, n, where):
        device = (x_pair, x_other)[where]
        source = order[k]
        return remote(
            relay.at[source, sub(n)], relay.at[source, sub(n)],
            sq.at[k % 2, where, n], rq.at[source, n], device,
        )

    def bt_sub(half, u, n):
        start = pl.multiple_of(half * HALF + u * PIECE + n * SUB, SUB)
        return bt.at[pl.ds(start, SUB)]

    def along_y(target, n):
        return remote(
            relay.at[target, sub(n)], bt_sub(core, y, n),
            sy.at[target, n], ry.at[y, n], (zh * 4 + target, col),
        )

    def stay(n):
        return pltpu.make_async_copy(relay.at[y, sub(n)], bt_sub(core, y, n), ry.at[y, n])

    def y_arrival(u, n):
        return remote(mine_t.at[sub(n)], bt_sub(core, u, n), sy.at[u, n], ry.at[u, n], sibling)

    def core_copy(u, n):
        return remote(
            bt_sub(core, u, n), bt_sub(core, u, n), sc.at[u, n], rc.at[u, n], sibling
        )

    def core_arrival(u, n):
        return remote(
            mine_t.at[sub(n)], bt_sub(1 - core, u, n), sc.at[u, n], rc.at[u, n], sibling
        )

    def give_y(target, n):
        @pl.when(target != y)
        def _():
            along_y(target, n).start()

        @pl.when(target == y)
        def _():
            stay(n).start()

    def over_z(k, n):
        source = order[k]
        return remote(
            relay.at[source, sub(n)], relay.at[source, sub(n)],
            sv.at[k // 2, n], rq.at[source, n], z_near,
        )

    def hand_out(k):
        for n in range(NSUB if k == 0 else OVER_Z):
            along_x(k, n, 0).start()
            along_x(k, n, 1).start()
        for n in range(NSUB):
            give_y(order[k], n)

    def pass_on(m):
        k, n = m // NSUB, m % NSUB

        @pl.when(jnp.logical_not(home))
        def _():
            along_x(k, n, 0).wait_recv()
            if k == 0 or n < OVER_Z:
                along_x(k, n, 0).start()
            if k == 0 and n >= OVER_Z:
                over_z(k, n).start()
            give_y(order[k], n)

    def take_in(m):
        k, n = 2 + m // NSUB, m % NSUB
        along_x(k, n, 0).wait_recv()
        if k == 2 and n >= OVER_Z:
            over_z(k, n).start()
        give_y(order[k], n)

    def cross(m):
        u, n = m // NSUB, m % NSUB
        y_arrival(u, n).wait_recv()
        core_copy(u, n).start()

    for i in range(AHEAD):
        x_copy(i).start()
    for i in range(NCH):
        own_copy(i).start()

    loads[0].wait()
    piece_cols = pl.ds(pl.multiple_of(y * PIECE, PIECE), PIECE)
    for i in range(NB // PIECE):
        rows = pl.ds(i * PIECE, PIECE)
        mine_t[:, rows] = b_own[rows, piece_cols].astype(F32).T.astype(BF16)

    @pl.when(home)
    def _():
        near_half().start()
        for n in range(NSUB):
            held_copy(n).start()
        for n in range(NSUB):
            held_copy(n).wait()
        hand_out(0)

    @pl.when(jnp.logical_not(home))
    def _():
        mirror_half().start()

    col_source = (block + 4) % 8
    row_source = (row + 4) % 8
    lines = lax.broadcasted_iota(jnp.int32, (8, NB), 0)

    def line(table, wanted):
        return jnp.sum(jnp.where(lines == wanted, table[...], 0), axis=0, keepdims=True)

    perm_row[0:1, :] = line(perm, col_source)
    perm_row[1:2, :] = line(perm, row_source)
    perm_row[2:3, :] = line(perm, row)
    scale_row[0:1, :] = line(scale, col_source)
    scale_row[1:2, :] = line(scale, row)

    half_cols = pl.ds(pl.multiple_of(core * HALF, HALF), HALF)

    @pl.loop(0, NB // 128)
    def _(i):
        rows = pl.ds(i * 128, 128)
        wanted = perm_row[0:1, half_cols]
        here = lax.broadcasted_iota(jnp.int32, (128, HALF), 0) + i * 128
        onehot[rows, :] = jnp.where(here == wanted, 1.0, 0.0).astype(BF16)

    for i in range(NB // 128):
        part_row = perm_row[1:2, pl.ds(i * 128, 128)]
        perm_col[pl.ds(i * 128, 128), :] = jnp.broadcast_to(part_row, (128, 128)).T

    @pl.loop(0, NB // 128)
    def _(i):
        here = lax.broadcasted_iota(jnp.int32, (128, NB), 0) + i * 128
        hit = jnp.where(here == perm_row[2:3, :], scale_row[1:2, :], 0.0)
        place = pl.ds(pl.multiple_of((i % 8) * 128, 128), 128)
        lanes = pl.ds(pl.multiple_of((i // 8) * 128, 128), 128)
        inv_scale[place, lanes] = jnp.broadcast_to(
            jnp.sum(hit, axis=1, keepdims=True), (128, 128)
        )

    def gathered(rows, i):
        wanted = perm_col[rows, :]
        wanted = jnp.concatenate([wanted, wanted], axis=1)
        here = lax.broadcasted_iota(jnp.int32, (CH, CH), 1) + i * CH
        pick = jnp.where(here == wanted, 1.0, 0.0).astype(BF16)
        far = marr[pl.ds(pl.multiple_of(i * CH, CH), CH), :]
        return jnp.dot(pick, far, preferred_element_type=F32)

    def add_matched(i):
        z_copy(i).wait_recv()

        @pl.loop(0, NCH)
        def _(t):
            rows = pl.ds(pl.multiple_of(t * CH, CH), CH)
            far = gathered(rows, i)

            @pl.when(i == 0)
            def _():
                acc[rows, :] = far

            @pl.when(i > 0)
            def _():
                acc[rows, :] += far

    @pl.when(home)
    def _():
        near_half().wait_recv()
        mirror_half().wait_recv()
        hand_out(1)

    @pl.loop(0, NCH)
    def _(i):
        rows = pl.ds(pl.multiple_of(i * CH, CH), CH)

        @pl.when(i + AHEAD < NCH)
        def _():
            x_copy(i + AHEAD).start()

        x_copy(i).wait_recv()
        forward(i).start()

        own_load(i).wait()
        own_arrival(i).wait_recv()
        forward_arrival(i).wait_recv()

        @pl.loop(0, HALF // 256)
        def _(n):
            cols = pl.ds(pl.multiple_of(n * 256, 256), 256)
            value = jnp.dot(s_own[0, rows, :], b_own[:HALF, cols], preferred_element_type=F32)
            value += jnp.dot(s_own[1, rows, :], b_own[HALF:, cols], preferred_element_type=F32)
            moved = jnp.dot(s_par[0, rows, :], onehot[:HALF, cols], preferred_element_type=F32)
            moved += jnp.dot(s_par[1, rows, :], onehot[HALF:, cols], preferred_element_type=F32)
            here = pl.ds(pl.multiple_of(core * HALF + n * 256, 256), 256)
            value += moved * scale_row[0:1, here]
            value = value.astype(BF16)
            mixed[rows, cols] = value
            lanes = inv_scale[
                pl.ds(pl.multiple_of((i % 4) * CH, CH), CH),
                pl.ds(pl.multiple_of((i // 4) * 128, 128), 128),
            ]
            sent[rows, cols] = (
                value.astype(F32) * jnp.concatenate([lanes, lanes], axis=1)
            ).astype(BF16)

        z_copy(i).start()

        for step in range(NCH):
            if PASS_AT[step] or TAKE_AT[step]:
                @pl.when(i == step)
                def _():
                    for m in PASS_AT[step]:
                        pass_on(m)
                    for m in TAKE_AT[step]:
                        take_in(m)

        @pl.when(i >= LAG)
        def _():
            add_matched(i - LAG)

    for m in AFTER_PASS:
        pass_on(m)
    for m in AFTER_TAKE:
        take_in(m)
    for m in range(4 * NSUB):
        cross(m)

    @pl.loop(0, NCH)
    def _(step):
        u = step // 2
        half = lax.rem(step + core, 2)
        rows = pl.ds(pl.multiple_of((half * (NCH // 2) + u) * CH, CH), CH)

        @pl.when(half != core)
        def _():
            for n in range(NSUB):
                core_arrival(u, n).wait_recv()

        @pl.loop(0, HALF // 512)
        def _(n):
            cols = pl.ds(pl.multiple_of(n * 512, 512), 512)
            acc[rows, cols] += jnp.dot(bt[rows, :], mixed[:, cols], preferred_element_type=F32)

    for i in range(NCH - LAG, NCH - 1):
        add_matched(i)
    z_copy(NCH - 1).wait_recv()

    loads[1].wait()
    offset = col * HALF - row * NB

    def out_copy(t):
        rows = pl.ds(pl.multiple_of(t * CH, CH), CH)
        return pltpu.make_async_copy(sent.at[rows], new_sim.at[rows], out_sem.at[t])

    def line_of(t):
        return pl.ds(pl.multiple_of(t * 128, 128), 128)

    def give_copy(t):
        rows = pl.ds(pl.multiple_of(t * CH + (1 - core) * 128, 128), 128)
        return remote(
            acc.at[rows, pl.ds(0, F)], inv_scale.at[line_of(t)], sp.at[t], rp.at[t], sibling
        )

    def part_copy(t):
        device = (row, 2 * t + core)
        return remote(part.at[line_of(t)], slots.at[block], sa.at[t], ra.at[block], device)

    def part_arrival(i):
        return remote(part.at[line_of(0)], slots.at[i], sa.at[i], ra.at[i], sibling)

    def settle(t):
        give_copy(t).wait_recv()
        rows = pl.ds(pl.multiple_of(t * CH + core * 128, 128), 128)
        kept = acc[rows, pl.ds(0, F)] + inv_scale[line_of(t), :]

        @pl.when(t != block)
        def _():
            part[line_of(t), :] = kept.astype(BF16)
            part_copy(t).start()

        @pl.when(t == block)
        def _():
            total[...] = kept

    @pl.loop(0, NCH)
    def _(i):
        z_copy(i).wait_send()

    @pl.loop(0, NCH)
    def _(step):
        t = (step + block + 1) % NCH
        rows = pl.ds(pl.multiple_of(t * CH, CH), CH)
        value = decay_factor * (acc[rows, :] + gathered(rows, NCH - 1))
        down = lax.broadcasted_iota(jnp.int32, (CH, HALF), 0) + t * CH
        across = lax.broadcasted_iota(jnp.int32, (CH, HALF), 1) + offset
        value = jnp.where(down == across, 1.0, value).astype(BF16)
        sent[rows, :] = value
        out_copy(t).start()
        acc[rows, pl.ds(0, F)] = jnp.dot(value, feats[...], preferred_element_type=F32)
        give_copy(t).start()

        @pl.when(step > 0)
        def _():
            settle((step + block) % NCH)

    settle(block)

    @pl.loop(1, NCH)
    def _(i):
        source = (block + NCH - i) % NCH
        part_arrival(source).wait_recv()
        total[...] += slots[source].astype(F32)

    agg_copy = pltpu.make_async_copy(total, agg, agg_sem)
    agg_copy.start()

    @pl.loop(0, NCH)
    def _(i):
        x_copy(i).wait_send()
        own_copy(i).wait_send()
        forward(i).wait_send()
        out_copy(i).wait()

    for n in range(NSUB):
        for u in range(4):
            core_copy(u, n).wait_send()

            @pl.when(u != y)
            def _():
                along_y(u, n).wait_send()

        if n >= OVER_Z:
            over_z(2, n).wait_send()

            @pl.when(jnp.logical_not(home))
            def _():
                over_z(0, n).wait_send()

        for k in range(2):
            if k == 0 or n < OVER_Z:
                along_x(k, n, 0).wait_send()

                @pl.when(home)
                def _():
                    along_x(k, n, 1).wait_send()

    @pl.when(home)
    def _():
        near_half().wait_send()

    @pl.when(jnp.logical_not(home))
    def _():
        mirror_half().wait_send()

    @pl.loop(0, NCH)
    def _(t):
        give_copy(t).wait_send()

        @pl.when(t != block)
        def _():
            part_copy(t).wait_send()

    agg_copy.wait()


def on_device(sim, diag_blocks, match_perm, match_scale, features):
    dma = pltpu.SemaphoreType.DMA
    return pl.pallas_call(
        kernel,
        out_shape=(
            jax.ShapeDtypeStruct((NB, HALF), BF16),
            jax.ShapeDtypeStruct((128, F), F32),
            jax.ShapeDtypeStruct((4, PIECE, NB), BF16),
        ),
        in_specs=[
            pl.BlockSpec(memory_space=pl.ANY),
            pl.BlockSpec(memory_space=pl.ANY),
            pl.BlockSpec(memory_space=pltpu.VMEM),
            pl.BlockSpec(memory_space=pltpu.VMEM),
            pl.BlockSpec(memory_space=pl.ANY),
        ],
        out_specs=(
            pl.BlockSpec(memory_space=pl.ANY),
            pl.BlockSpec(memory_space=pl.ANY),
            pl.BlockSpec(memory_space=pl.ANY),
        ),
        scratch_shapes=[
            pltpu.VMEM((2, NB, HALF), BF16),
            pltpu.VMEM((2, NB, HALF), BF16),
            pltpu.VMEM((NB, HALF), BF16),
            pltpu.VMEM((NB, HALF), BF16),
            pltpu.VMEM((NB, HALF), BF16),
            pltpu.VMEM((NB, HALF), BF16),
            pltpu.VMEM((NB, HALF), BF16),
            pltpu.VMEM((NB, NB), BF16),
            pltpu.VMEM((NB, HALF), F32),
            pltpu.VMEM((HALF, F), BF16),
            pltpu.VMEM((PIECE, NB), BF16),
            pltpu.VMEM((8, NB), jnp.int32),
            pltpu.VMEM((8, NB), F32),
            pltpu.VMEM((NB, 128), jnp.int32),
            pltpu.VMEM((HALF, 256), F32),
            pltpu.VMEM((HALF, F), BF16),
            pltpu.VMEM((8, 128, F), BF16),
            pltpu.VMEM((128, F), F32),
            dma((2,)), dma((NCH,)),
            dma((NCH,)), dma((NCH,)),
            dma((NCH,)), dma((NCH,)),
            dma((NCH,)), dma((NCH,)),
            dma((NCH,)), dma((NCH,)),
            dma((2,)), dma((2,)),
            dma((2, 2, NSUB)), dma((4, NSUB)), dma((2, NSUB)),
            dma((4, NSUB)), dma((4, NSUB)),
            dma((4, NSUB)), dma((4, NSUB)),
            dma((8,)), dma((8,)),
            dma((8,)), dma((8,)),
            dma((NCH,)), dma(()),
        ],
        compiler_params=pltpu.CompilerParams(
            collective_id=0, has_side_effects=True, vmem_limit_bytes=60 * 2**20
        ),
        name="simrank",
    )(sim, diag_blocks, match_perm, match_scale, features)[:2]


def solution(mesh):
    placed = (P("row", "col"), P(None, "col"), P(), P(), P("col", None))
    return jax.shard_map(
        on_device,
        mesh=mesh,
        in_specs=placed,
        out_specs=(P("row", "col"), P(("row", "col"), None)),
        check_vma=False,
    )
```

```python
import jax
import jax.numpy as jnp
from jax import lax
from jax.experimental import pallas as pl
from jax.experimental.pallas import tpu as pltpu
from jax.sharding import PartitionSpec as P

decay_factor = 0.8
MESH = pl.DeviceIdType.MESH

NB = 2048
HALF = 1024
F = 256
CH = 256
NCH = NB // CH
PIECE = 256
NSUB = 4
OVER_Z = 2
SUB = PIECE // NSUB
AHEAD = 2
LAG = 2
PASS_AT = ((0, 1, 2, 3), (4, 5, 6, 7), (), (), (), (), (), ())
TAKE_AT = ((0, 1), (2, 3, 4), (5, 6, 7), (), (), (), (), ())
AFTER_PASS = ()
AFTER_TAKE = ()
BF16 = jnp.bfloat16
F32 = jnp.float32


def kernel(
    sim, diag, perm, scale, feat,
    new_sim, agg, relay,
    s_own, s_par, b_own, onehot, mixed, sent, marr, bt, acc, feats,
    mine_t, perm_row, scale_row, perm_col, inv_scale, part, slots, total,
    load_sem, own_sem,
    sx, rx, sz, rz, sd, rd, sf, rf, sb, rb, sq, rq, sv, sy, ry, sc, rc, sp, rp, sa, ra, out_sem, agg_sem,
):
    row = lax.axis_index("row")
    col = lax.axis_index("col")
    zh, y = row // 4, row % 4
    x, zl, core = col // 4, (col // 2) % 2, col % 2
    block = col // 2
    sibling = (row, col + 1 - 2 * core)
    x_partner = (row, (col + 8) % 16)
    z_partner = ((row + 4) % 8, col)
    z_near = (row, col + 2 - 4 * zl)
    z_mirror = ((1 - zh) * 4 + y, x * 4 + (1 - zl) * 2 + core)
    x_pair = (row, col + 4 - 8 * (x % 2))
    x_other = (row, (col + 12 + 8 * (x % 2)) % 16)
    home = x // 2 == zh
    home_int = home.astype(jnp.int32)
    pair = 2 * lax.rem(x + 1 - home_int, 2)
    order = (pair + zl, pair + 1 - zl, 2 - pair + zl, 3 - pair - zl)
    held = 2 * (x % 2) + zl

    barrier = pltpu.get_barrier_semaphore()

    def greet(device):
        pl.semaphore_signal(barrier, inc=1, device_id=device, device_id_type=MESH)

    for i in range(1, 16):
        greet((row, (col + i) % 16))
    for i in range(1, 4):
        greet((zh * 4 + (y + i) % 4, col))
    greet(z_partner)
    greet(z_mirror)

    loads = [
        pltpu.make_async_copy(diag, b_own, load_sem.at[0]),
        pltpu.make_async_copy(feat, feats, load_sem.at[1]),
    ]
    for load in loads:
        load.start()

    def own_load(i):
        rows = pl.ds(i * CH, CH)
        return pltpu.make_async_copy(
            sim.at[rows], s_own.at[core, rows], own_sem.at[i]
        )

    for i in range(NCH):
        own_load(i).start()
    pl.semaphore_wait(barrier, 20)

    def remote(src, dst, send, recv, device):
        return pltpu.make_async_remote_copy(
            src_ref=src, dst_ref=dst, send_sem=send, recv_sem=recv,
            device_id=device, device_id_type=MESH,
        )

    def x_copy(i):
        rows = pl.ds(i * CH, CH)
        return remote(sim.at[rows], s_par.at[core, rows], sx.at[i], rx.at[i], x_partner)

    def own_copy(i):
        rows = pl.ds(i * CH, CH)
        return remote(sim.at[rows], s_own.at[core, rows], sd.at[i], rd.at[i], sibling)

    def own_arrival(i):
        rows = pl.ds(i * CH, CH)
        return remote(sim.at[rows], s_own.at[1 - core, rows], sd.at[i], rd.at[i], sibling)

    def forward(i):
        rows = pl.ds(i * CH, CH)
        return remote(s_par.at[core, rows], s_par.at[core, rows], sf.at[i], rf.at[i], sibling)

    def forward_arrival(i):
        rows = pl.ds(i * CH, CH)
        return remote(s_par.at[core, rows], s_par.at[1 - core, rows], sf.at[i], rf.at[i], sibling)

    def z_copy(i):
        rows = pl.ds(i * CH, CH)
        return remote(sent.at[rows], marr.at[rows], sz.at[i], rz.at[i], z_partner)

    def bt_rows(half, part_of):
        return bt.at[pl.ds(pl.multiple_of(half * HALF + part_of * PIECE, PIECE), PIECE)]

    def near_half():
        rows = pl.ds(0, PIECE // 2)
        return remote(
            mine_t.at[rows], relay.at[held, rows], sb.at[0], rb.at[0], z_near
        )

    def mirror_half():
        rows = pl.ds(PIECE // 2, PIECE // 2)
        return remote(
            mine_t.at[rows], relay.at[held, rows], sb.at[1], rb.at[1], z_mirror
        )

    def held_copy(n):
        rows = pl.ds(n * SUB, SUB)
        return pltpu.make_async_copy(mine_t.at[rows], relay.at[held, rows], rq.at[held, n])

    def sub(n):
        return pl.ds(n * SUB, SUB)

    def along_x(k, n, where):
        device = (x_pair, x_other)[where]
        source = order[k]
        return remote(
            relay.at[source, sub(n)], relay.at[source, sub(n)],
            sq.at[k % 2, where, n], rq.at[source, n], device,
        )

    def bt_sub(half, u, n):
        start = pl.multiple_of(half * HALF + u * PIECE + n * SUB, SUB)
        return bt.at[pl.ds(start, SUB)]

    def along_y(target, n):
        return remote(
            relay.at[target, sub(n)], bt_sub(core, y, n),
            sy.at[target, n], ry.at[y, n], (zh * 4 + target, col),
        )

    def stay(n):
        return pltpu.make_async_copy(relay.at[y, sub(n)], bt_sub(core, y, n), ry.at[y, n])

    def y_arrival(u, n):
        return remote(mine_t.at[sub(n)], bt_sub(core, u, n), sy.at[u, n], ry.at[u, n], sibling)

    def core_copy(u, n):
        return remote(
            bt_sub(core, u, n), bt_sub(core, u, n), sc.at[u, n], rc.at[u, n], sibling
        )

    def core_arrival(u, n):
        return remote(
            mine_t.at[sub(n)], bt_sub(1 - core, u, n), sc.at[u, n], rc.at[u, n], sibling
        )

    def give_y(target, n):
        @pl.when(target != y)
        def _():
            along_y(target, n).start()

        @pl.when(target == y)
        def _():
            stay(n).start()

    def over_z(k, n):
        source = order[k]
        return remote(
            relay.at[source, sub(n)], relay.at[source, sub(n)],
            sv.at[k // 2, n], rq.at[source, n], z_near,
        )

    def hand_out(k):
        for n in range(NSUB if k == 0 else OVER_Z):
            along_x(k, n, 0).start()
            along_x(k, n, 1).start()
        for n in range(NSUB):
            give_y(order[k], n)

    def pass_on(m):
        k, n = m // NSUB, m % NSUB

        @pl.when(jnp.logical_not(home))
        def _():
            along_x(k, n, 0).wait_recv()
            if k == 0 or n < OVER_Z:
                along_x(k, n, 0).start()
            if k == 0 and n >= OVER_Z:
                over_z(k, n).start()
            give_y(order[k], n)

    def take_in(m):
        k, n = 2 + m // NSUB, m % NSUB
        along_x(k, n, 0).wait_recv()
        if k == 2 and n >= OVER_Z:
            over_z(k, n).start()
        give_y(order[k], n)

    def cross(m):
        u, n = m // NSUB, m % NSUB
        y_arrival(u, n).wait_recv()
        core_copy(u, n).start()

    for i in range(AHEAD):
        x_copy(i).start()
    for i in range(NCH):
        own_copy(i).start()

    loads[0].wait()
    piece_cols = pl.ds(pl.multiple_of(y * PIECE, PIECE), PIECE)
    for i in range(NB // PIECE):
        rows = pl.ds(i * PIECE, PIECE)
        mine_t[:, rows] = b_own[rows, piece_cols].astype(F32).T.astype(BF16)

    @pl.when(home)
    def _():
        near_half().start()
        for n in range(NSUB):
            held_copy(n).start()
        for n in range(NSUB):
            held_copy(n).wait()
        hand_out(0)

    @pl.when(jnp.logical_not(home))
    def _():
        mirror_half().start()

    col_source = (block + 4) % 8
    row_source = (row + 4) % 8
    lines = lax.broadcasted_iota(jnp.int32, (8, NB), 0)

    def line(table, wanted):
        return jnp.sum(jnp.where(lines == wanted, table[...], 0), axis=0, keepdims=True)

    perm_row[0:1, :] = line(perm, col_source)
    perm_row[1:2, :] = line(perm, row_source)
    perm_row[2:3, :] = line(perm, row)
    scale_row[0:1, :] = line(scale, col_source)
    scale_row[1:2, :] = line(scale, row)

    half_cols = pl.ds(pl.multiple_of(core * HALF, HALF), HALF)

    @pl.loop(0, NB // 128)
    def _(i):
        rows = pl.ds(i * 128, 128)
        wanted = perm_row[0:1, half_cols]
        here = lax.broadcasted_iota(jnp.int32, (128, HALF), 0) + i * 128
        onehot[rows, :] = jnp.where(here == wanted, 1.0, 0.0).astype(BF16)

    for i in range(NB // 128):
        part_row = perm_row[1:2, pl.ds(i * 128, 128)]
        perm_col[pl.ds(i * 128, 128), :] = jnp.broadcast_to(part_row, (128, 128)).T

    @pl.loop(0, NB // 128)
    def _(i):
        here = lax.broadcasted_iota(jnp.int32, (128, NB), 0) + i * 128
        hit = jnp.where(here == perm_row[2:3, :], scale_row[1:2, :], 0.0)
        place = pl.ds(pl.multiple_of((i % 8) * 128, 128), 128)
        lanes = pl.ds(pl.multiple_of((i // 8) * 128, 128), 128)
        inv_scale[place, lanes] = jnp.broadcast_to(
            jnp.sum(hit, axis=1, keepdims=True), (128, 128)
        )

    def gathered(rows, i):
        wanted = perm_col[rows, :]
        wanted = jnp.concatenate([wanted, wanted], axis=1)
        here = lax.broadcasted_iota(jnp.int32, (CH, CH), 1) + i * CH
        pick = jnp.where(here == wanted, 1.0, 0.0).astype(BF16)
        far = marr[pl.ds(pl.multiple_of(i * CH, CH), CH), :]
        return jnp.dot(pick, far, preferred_element_type=F32)

    def add_matched(i):
        z_copy(i).wait_recv()

        @pl.loop(0, NCH)
        def _(t):
            rows = pl.ds(pl.multiple_of(t * CH, CH), CH)
            far = gathered(rows, i)

            @pl.when(i == 0)
            def _():
                acc[rows, :] = far

            @pl.when(i > 0)
            def _():
                acc[rows, :] += far

    @pl.when(home)
    def _():
        near_half().wait_recv()
        mirror_half().wait_recv()
        hand_out(1)

    @pl.loop(0, NCH)
    def _(i):
        rows = pl.ds(pl.multiple_of(i * CH, CH), CH)

        @pl.when(i + AHEAD < NCH)
        def _():
            x_copy(i + AHEAD).start()

        x_copy(i).wait_recv()
        forward(i).start()

        own_load(i).wait()
        own_arrival(i).wait_recv()
        forward_arrival(i).wait_recv()

        @pl.loop(0, HALF // 256)
        def _(n):
            cols = pl.ds(pl.multiple_of(n * 256, 256), 256)
            value = jnp.dot(s_own[0, rows, :], b_own[:HALF, cols], preferred_element_type=F32)
            value += jnp.dot(s_own[1, rows, :], b_own[HALF:, cols], preferred_element_type=F32)
            moved = jnp.dot(s_par[0, rows, :], onehot[:HALF, cols], preferred_element_type=F32)
            moved += jnp.dot(s_par[1, rows, :], onehot[HALF:, cols], preferred_element_type=F32)
            here = pl.ds(pl.multiple_of(core * HALF + n * 256, 256), 256)
            value += moved * scale_row[0:1, here]
            value = value.astype(BF16)
            mixed[rows, cols] = value
            lanes = inv_scale[
                pl.ds(pl.multiple_of((i % 4) * CH, CH), CH),
                pl.ds(pl.multiple_of((i // 4) * 128, 128), 128),
            ]
            sent[rows, cols] = (
                value.astype(F32) * jnp.concatenate([lanes, lanes], axis=1)
            ).astype(BF16)

        z_copy(i).start()

        for step in range(NCH):
            if PASS_AT[step] or TAKE_AT[step]:
                @pl.when(i == step)
                def _():
                    for m in PASS_AT[step]:
                        pass_on(m)
                    for m in TAKE_AT[step]:
                        take_in(m)

        @pl.when(i >= LAG)
        def _():
            add_matched(i - LAG)

    for m in AFTER_PASS:
        pass_on(m)
    for m in AFTER_TAKE:
        take_in(m)
    for m in range(4 * NSUB):
        cross(m)

    @pl.loop(0, NCH)
    def _(step):
        u = step // 2
        half = lax.rem(step + core, 2)
        rows = pl.ds(pl.multiple_of((half * (NCH // 2) + u) * CH, CH), CH)

        @pl.when(half != core)
        def _():
            for n in range(NSUB):
                core_arrival(u, n).wait_recv()

        @pl.loop(0, HALF // 512)
        def _(n):
            cols = pl.ds(pl.multiple_of(n * 512, 512), 512)
            acc[rows, cols] += jnp.dot(bt[rows, :], mixed[:, cols], preferred_element_type=F32)

    for i in range(NCH - LAG, NCH - 1):
        add_matched(i)
    z_copy(NCH - 1).wait_recv()

    loads[1].wait()
    offset = col * HALF - row * NB

    def out_copy(t):
        rows = pl.ds(pl.multiple_of(t * CH, CH), CH)
        return pltpu.make_async_copy(sent.at[rows], new_sim.at[rows], out_sem.at[t])

    def line_of(t):
        return pl.ds(pl.multiple_of(t * 128, 128), 128)

    def give_copy(t):
        rows = pl.ds(pl.multiple_of(t * CH + (1 - core) * 128, 128), 128)
        return remote(
            acc.at[rows, pl.ds(0, F)], inv_scale.at[line_of(t)], sp.at[t], rp.at[t], sibling
        )

    def part_copy(t):
        device = (row, 2 * t + core)
        return remote(part.at[line_of(t)], slots.at[block], sa.at[t], ra.at[block], device)

    def part_arrival(i):
        return remote(part.at[line_of(0)], slots.at[i], sa.at[i], ra.at[i], sibling)

    def settle(t):
        give_copy(t).wait_recv()
        rows = pl.ds(pl.multiple_of(t * CH + core * 128, 128), 128)
        kept = acc[rows, pl.ds(0, F)] + inv_scale[line_of(t), :]

        @pl.when(t != block)
        def _():
            part[line_of(t), :] = kept.astype(BF16)
            part_copy(t).start()

        @pl.when(t == block)
        def _():
            total[...] = kept

    @pl.loop(0, NCH)
    def _(i):
        z_copy(i).wait_send()

    @pl.loop(0, NCH)
    def _(step):
        t = (step + block + 1) % NCH
        rows = pl.ds(pl.multiple_of(t * CH, CH), CH)
        value = decay_factor * (acc[rows, :] + gathered(rows, NCH - 1))
        down = lax.broadcasted_iota(jnp.int32, (CH, HALF), 0) + t * CH
        across = lax.broadcasted_iota(jnp.int32, (CH, HALF), 1) + offset
        value = jnp.where(down == across, 1.0, value).astype(BF16)
        sent[rows, :] = value
        out_copy(t).start()
        acc[rows, pl.ds(0, F)] = jnp.dot(value, feats[...], preferred_element_type=F32)
        give_copy(t).start()

        @pl.when(step > 0)
        def _():
            settle((step + block) % NCH)

    settle(block)

    @pl.loop(1, NCH)
    def _(i):
        source = (block + NCH - i) % NCH
        part_arrival(source).wait_recv()
        total[...] += slots[source].astype(F32)

    agg_copy = pltpu.make_async_copy(total, agg, agg_sem)
    agg_copy.start()

    @pl.loop(0, NCH)
    def _(i):
        x_copy(i).wait_send()
        own_copy(i).wait_send()
        forward(i).wait_send()
        out_copy(i).wait()

    for n in range(NSUB):
        for u in range(4):
            core_copy(u, n).wait_send()

            @pl.when(u != y)
            def _():
                along_y(u, n).wait_send()

        if n >= OVER_Z:
            over_z(2, n).wait_send()

            @pl.when(jnp.logical_not(home))
            def _():
                over_z(0, n).wait_send()

        for k in range(2):
            if k == 0 or n < OVER_Z:
                along_x(k, n, 0).wait_send()

                @pl.when(home)
                def _():
                    along_x(k, n, 1).wait_send()

    @pl.when(home)
    def _():
        near_half().wait_send()

    @pl.when(jnp.logical_not(home))
    def _():
        mirror_half().wait_send()

    @pl.loop(0, NCH)
    def _(t):
        give_copy(t).wait_send()

        @pl.when(t != block)
        def _():
            part_copy(t).wait_send()

    agg_copy.wait()


def finish(made, summed, new_sim, agg, held, held_sum, into, out):
    rows = [pl.ds(i * (NB // 4), NB // 4) for i in range(4)]
    reads = [pltpu.make_async_copy(made.at[r], held.at[r], into.at[i]) for i, r in enumerate(rows)]
    reads.append(pltpu.make_async_copy(summed, held_sum, into.at[4]))
    writes = [pltpu.make_async_copy(held.at[r], new_sim.at[r], out.at[i]) for i, r in enumerate(rows)]
    writes.append(pltpu.make_async_copy(held_sum, agg, out.at[4]))
    for read in reads:
        read.start()
    for read, write in zip(reads, writes):
        read.wait()
        write.start()
    for write in writes:
        write.wait()


def on_device(sim, diag_blocks, match_perm, match_scale, features):
    dma = pltpu.SemaphoreType.DMA
    made, summed, _ = pl.pallas_call(
        kernel,
        out_shape=(
            jax.ShapeDtypeStruct((NB, HALF), BF16),
            jax.ShapeDtypeStruct((128, F), F32),
            jax.ShapeDtypeStruct((4, PIECE, NB), BF16),
        ),
        in_specs=[
            pl.BlockSpec(memory_space=pl.ANY),
            pl.BlockSpec(memory_space=pl.ANY),
            pl.BlockSpec(memory_space=pltpu.VMEM),
            pl.BlockSpec(memory_space=pltpu.VMEM),
            pl.BlockSpec(memory_space=pl.ANY),
        ],
        out_specs=(
            pl.BlockSpec(memory_space=pl.ANY),
            pl.BlockSpec(memory_space=pl.ANY),
            pl.BlockSpec(memory_space=pl.ANY),
        ),
        scratch_shapes=[
            pltpu.VMEM((2, NB, HALF), BF16),
            pltpu.VMEM((2, NB, HALF), BF16),
            pltpu.VMEM((NB, HALF), BF16),
            pltpu.VMEM((NB, HALF), BF16),
            pltpu.VMEM((NB, HALF), BF16),
            pltpu.VMEM((NB, HALF), BF16),
            pltpu.VMEM((NB, HALF), BF16),
            pltpu.VMEM((NB, NB), BF16),
            pltpu.VMEM((NB, HALF), F32),
            pltpu.VMEM((HALF, F), BF16),
            pltpu.VMEM((PIECE, NB), BF16),
            pltpu.VMEM((8, NB), jnp.int32),
            pltpu.VMEM((8, NB), F32),
            pltpu.VMEM((NB, 128), jnp.int32),
            pltpu.VMEM((HALF, 256), F32),
            pltpu.VMEM((HALF, F), BF16),
            pltpu.VMEM((8, 128, F), BF16),
            pltpu.VMEM((128, F), F32),
            dma((2,)), dma((NCH,)),
            dma((NCH,)), dma((NCH,)),
            dma((NCH,)), dma((NCH,)),
            dma((NCH,)), dma((NCH,)),
            dma((NCH,)), dma((NCH,)),
            dma((2,)), dma((2,)),
            dma((2, 2, NSUB)), dma((4, NSUB)), dma((2, NSUB)),
            dma((4, NSUB)), dma((4, NSUB)),
            dma((4, NSUB)), dma((4, NSUB)),
            dma((8,)), dma((8,)),
            dma((8,)), dma((8,)),
            dma((NCH,)), dma(()),
        ],
        compiler_params=pltpu.CompilerParams(
            collective_id=0, has_side_effects=True, vmem_limit_bytes=60 * 2**20
        ),
        name="simrank",
    )(sim, diag_blocks, match_perm, match_scale, features)
    hbm = pl.BlockSpec(memory_space=pl.ANY)
    return pl.pallas_call(
        finish,
        out_shape=(
            jax.ShapeDtypeStruct((NB, HALF), BF16),
            jax.ShapeDtypeStruct((128, F), F32),
        ),
        in_specs=[hbm, hbm],
        out_specs=(hbm, hbm),
        scratch_shapes=[
            pltpu.VMEM((NB, HALF), BF16),
            pltpu.VMEM((128, F), F32),
            dma((5,)),
            dma((5,)),
        ],
        name="finish",
    )(made, summed)


def solution(mesh):
    placed = (P("row", "col"), P(None, "col"), P(), P(), P("col", None))
    return jax.shard_map(
        on_device,
        mesh=mesh,
        in_specs=placed,
        out_specs=(P("row", "col"), P(("row", "col"), None)),
        check_vma=False,
    )
```

```python
import jax
import jax.numpy as jnp
from jax import lax
from jax.experimental import pallas as pl
from jax.experimental.pallas import tpu as pltpu
from jax.sharding import PartitionSpec as P

decay_factor = 0.8
MESH = pl.DeviceIdType.MESH

NB = 2048
HALF = 1024
F = 256
CH = 256
NCH = NB // CH
PIECE = 256
NSUB = 4
OVER_Z = 2
SUB = PIECE // NSUB
AHEAD = 2
LAG = 2
PASS_AT = ((0, 1, 2, 3), (4, 5, 6, 7), (), (), (), (), (), ())
TAKE_AT = ((), (0, 1, 2, 3), (4, 5, 6, 7), (), (), (), (), ())
AFTER_PASS = ()
AFTER_TAKE = ()
BF16 = jnp.bfloat16
F32 = jnp.float32


def kernel(
    sim, diag, perm, scale, feat,
    new_sim, agg, relay,
    s_own, s_par, b_own, onehot, mixed, sent, marr, bt, acc, feats,
    mine_t, perm_row, scale_row, perm_col, inv_scale, part, slots, total,
    load_sem, own_sem,
    sx, rx, sz, rz, sd, rd, sf, rf, sb, rb, sq, rq, sv, sy, ry, sc, rc, sp, rp, sa, ra, out_sem, agg_sem,
):
    row = lax.axis_index("row")
    col = lax.axis_index("col")
    zh, y = row // 4, row % 4
    x, zl, core = col // 4, (col // 2) % 2, col % 2
    block = col // 2
    sibling = (row, col + 1 - 2 * core)
    x_partner = (row, (col + 8) % 16)
    z_partner = ((row + 4) % 8, col)
    z_near = (row, col + 2 - 4 * zl)
    z_mirror = ((1 - zh) * 4 + y, x * 4 + (1 - zl) * 2 + core)
    x_pair = (row, col + 4 - 8 * (x % 2))
    x_other = (row, (col + 12 + 8 * (x % 2)) % 16)
    home = x // 2 == zh
    home_int = home.astype(jnp.int32)
    pair = 2 * lax.rem(x + 1 - home_int, 2)
    order = (pair + zl, pair + 1 - zl, 2 - pair + zl, 3 - pair - zl)
    held = 2 * (x % 2) + zl

    barrier = pltpu.get_barrier_semaphore()

    def greet(device):
        pl.semaphore_signal(barrier, inc=1, device_id=device, device_id_type=MESH)

    for i in range(1, 16):
        greet((row, (col + i) % 16))
    for i in range(1, 4):
        greet((zh * 4 + (y + i) % 4, col))
    greet(z_partner)
    greet(z_mirror)

    loads = [
        pltpu.make_async_copy(diag, b_own, load_sem.at[0]),
        pltpu.make_async_copy(feat, feats, load_sem.at[1]),
    ]
    for load in loads:
        load.start()

    def own_load(i):
        rows = pl.ds(i * CH, CH)
        return pltpu.make_async_copy(
            sim.at[rows], s_own.at[core, rows], own_sem.at[i]
        )

    for i in range(NCH):
        own_load(i).start()
    pl.semaphore_wait(barrier, 20)

    def remote(src, dst, send, recv, device):
        return pltpu.make_async_remote_copy(
            src_ref=src, dst_ref=dst, send_sem=send, recv_sem=recv,
            device_id=device, device_id_type=MESH,
        )

    def x_copy(i):
        rows = pl.ds(i * CH, CH)
        return remote(sim.at[rows], s_par.at[core, rows], sx.at[i], rx.at[i], x_partner)

    def own_copy(i):
        rows = pl.ds(i * CH, CH)
        return remote(sim.at[rows], s_own.at[core, rows], sd.at[i], rd.at[i], sibling)

    def own_arrival(i):
        rows = pl.ds(i * CH, CH)
        return remote(sim.at[rows], s_own.at[1 - core, rows], sd.at[i], rd.at[i], sibling)

    def forward(i):
        rows = pl.ds(i * CH, CH)
        return remote(s_par.at[core, rows], s_par.at[core, rows], sf.at[i], rf.at[i], sibling)

    def forward_arrival(i):
        rows = pl.ds(i * CH, CH)
        return remote(s_par.at[core, rows], s_par.at[1 - core, rows], sf.at[i], rf.at[i], sibling)

    def z_copy(i):
        rows = pl.ds(i * CH, CH)
        return remote(sent.at[rows], marr.at[rows], sz.at[i], rz.at[i], z_partner)

    def bt_rows(half, part_of):
        return bt.at[pl.ds(pl.multiple_of(half * HALF + part_of * PIECE, PIECE), PIECE)]

    def near_half():
        rows = pl.ds(0, PIECE // 2)
        return remote(
            mine_t.at[rows], relay.at[held, rows], sb.at[0], rb.at[0], z_near
        )

    def mirror_half():
        rows = pl.ds(PIECE // 2, PIECE // 2)
        return remote(
            mine_t.at[rows], relay.at[held, rows], sb.at[1], rb.at[1], z_mirror
        )

    def held_copy(n):
        rows = pl.ds(n * SUB, SUB)
        return pltpu.make_async_copy(mine_t.at[rows], relay.at[held, rows], rq.at[held, n])

    def sub(n):
        return pl.ds(n * SUB, SUB)

    def along_x(k, n, where):
        device = (x_pair, x_other)[where]
        source = order[k]
        return remote(
            relay.at[source, sub(n)], relay.at[source, sub(n)],
            sq.at[k % 2, where, n], rq.at[source, n], device,
        )

    def bt_sub(half, u, n):
        start = pl.multiple_of(half * HALF + u * PIECE + n * SUB, SUB)
        return bt.at[pl.ds(start, SUB)]

    def along_y(target, n):
        return remote(
            relay.at[target, sub(n)], bt_sub(core, y, n),
            sy.at[target, n], ry.at[y, n], (zh * 4 + target, col),
        )

    def stay(n):
        return pltpu.make_async_copy(relay.at[y, sub(n)], bt_sub(core, y, n), ry.at[y, n])

    def y_arrival(u, n):
        return remote(mine_t.at[sub(n)], bt_sub(core, u, n), sy.at[u, n], ry.at[u, n], sibling)

    def core_copy(u, n):
        return remote(
            bt_sub(core, u, n), bt_sub(core, u, n), sc.at[u, n], rc.at[u, n], sibling
        )

    def core_arrival(u, n):
        return remote(
            mine_t.at[sub(n)], bt_sub(1 - core, u, n), sc.at[u, n], rc.at[u, n], sibling
        )

    def give_y(target, n):
        @pl.when(target != y)
        def _():
            along_y(target, n).start()

        @pl.when(target == y)
        def _():
            stay(n).start()

    def over_z(k, n):
        source = order[k]
        return remote(
            relay.at[source, sub(n)], relay.at[source, sub(n)],
            sv.at[k // 2, n], rq.at[source, n], z_near,
        )

    def hand_out(k):
        for n in range(NSUB if k == 0 else OVER_Z):
            along_x(k, n, 0).start()
            along_x(k, n, 1).start()
        for n in range(NSUB):
            give_y(order[k], n)

    def pass_on(m):
        k, n = m // NSUB, m % NSUB

        @pl.when(jnp.logical_not(home))
        def _():
            along_x(k, n, 0).wait_recv()
            if k == 0 or n < OVER_Z:
                along_x(k, n, 0).start()
            if k == 0 and n >= OVER_Z:
                over_z(k, n).start()
            give_y(order[k], n)

    def take_in(m):
        k, n = 2 + m // NSUB, m % NSUB
        along_x(k, n, 0).wait_recv()
        if k == 2 and n >= OVER_Z:
            over_z(k, n).start()
        give_y(order[k], n)

    def cross(m):
        u, n = m // NSUB, m % NSUB
        y_arrival(u, n).wait_recv()
        core_copy(u, n).start()

    for i in range(AHEAD):
        x_copy(i).start()
    for i in range(NCH):
        own_copy(i).start()

    loads[0].wait()
    piece_cols = pl.ds(pl.multiple_of(y * PIECE, PIECE), PIECE)
    for i in range(NB // PIECE):
        rows = pl.ds(i * PIECE, PIECE)
        mine_t[:, rows] = b_own[rows, piece_cols].astype(F32).T.astype(BF16)

    @pl.when(home)
    def _():
        near_half().start()
        for n in range(NSUB):
            held_copy(n).start()
        for n in range(NSUB):
            held_copy(n).wait()
        hand_out(0)

    @pl.when(jnp.logical_not(home))
    def _():
        mirror_half().start()

    col_source = (block + 4) % 8
    row_source = (row + 4) % 8
    lines = lax.broadcasted_iota(jnp.int32, (8, NB), 0)

    def line(table, wanted):
        return jnp.sum(jnp.where(lines == wanted, table[...], 0), axis=0, keepdims=True)

    perm_row[0:1, :] = line(perm, col_source)
    perm_row[1:2, :] = line(perm, row_source)
    perm_row[2:3, :] = line(perm, row)
    scale_row[0:1, :] = line(scale, col_source)
    scale_row[1:2, :] = line(scale, row)

    half_cols = pl.ds(pl.multiple_of(core * HALF, HALF), HALF)

    @pl.loop(0, NB // 128)
    def _(i):
        rows = pl.ds(i * 128, 128)
        wanted = perm_row[0:1, half_cols]
        here = lax.broadcasted_iota(jnp.int32, (128, HALF), 0) + i * 128
        onehot[rows, :] = jnp.where(here == wanted, 1.0, 0.0).astype(BF16)

    for i in range(NB // 128):
        part_row = perm_row[1:2, pl.ds(i * 128, 128)]
        perm_col[pl.ds(i * 128, 128), :] = jnp.broadcast_to(part_row, (128, 128)).T

    @pl.loop(0, NB // 128)
    def _(i):
        here = lax.broadcasted_iota(jnp.int32, (128, NB), 0) + i * 128
        hit = jnp.where(here == perm_row[2:3, :], scale_row[1:2, :], 0.0)
        place = pl.ds(pl.multiple_of((i % 8) * 128, 128), 128)
        lanes = pl.ds(pl.multiple_of((i // 8) * 128, 128), 128)
        inv_scale[place, lanes] = jnp.broadcast_to(
            jnp.sum(hit, axis=1, keepdims=True), (128, 128)
        )

    def gathered(rows, i):
        wanted = perm_col[rows, :]
        wanted = jnp.concatenate([wanted, wanted], axis=1)
        here = lax.broadcasted_iota(jnp.int32, (CH, CH), 1) + i * CH
        pick = jnp.where(here == wanted, 1.0, 0.0).astype(BF16)
        far = marr[pl.ds(pl.multiple_of(i * CH, CH), CH), :]
        return jnp.dot(pick, far, preferred_element_type=F32)

    def add_matched(i):
        z_copy(i).wait_recv()

        @pl.loop(0, NCH)
        def _(t):
            rows = pl.ds(pl.multiple_of(t * CH, CH), CH)
            far = gathered(rows, i)

            @pl.when(i == 0)
            def _():
                acc[rows, :] = far

            @pl.when(i > 0)
            def _():
                acc[rows, :] += far

    @pl.when(home)
    def _():
        near_half().wait_recv()
        mirror_half().wait_recv()
        hand_out(1)

    @pl.loop(0, NCH)
    def _(i):
        rows = pl.ds(pl.multiple_of(i * CH, CH), CH)

        @pl.when(i + AHEAD < NCH)
        def _():
            x_copy(i + AHEAD).start()

        x_copy(i).wait_recv()
        forward(i).start()

        own_load(i).wait()
        own_arrival(i).wait_recv()
        forward_arrival(i).wait_recv()

        @pl.loop(0, HALF // 256)
        def _(n):
            cols = pl.ds(pl.multiple_of(n * 256, 256), 256)
            value = jnp.dot(s_own[0, rows, :], b_own[:HALF, cols], preferred_element_type=F32)
            value += jnp.dot(s_own[1, rows, :], b_own[HALF:, cols], preferred_element_type=F32)
            moved = jnp.dot(s_par[0, rows, :], onehot[:HALF, cols], preferred_element_type=F32)
            moved += jnp.dot(s_par[1, rows, :], onehot[HALF:, cols], preferred_element_type=F32)
            here = pl.ds(pl.multiple_of(core * HALF + n * 256, 256), 256)
            value += moved * scale_row[0:1, here]
            value = value.astype(BF16)
            mixed[rows, cols] = value
            lanes = inv_scale[
                pl.ds(pl.multiple_of((i % 4) * CH, CH), CH),
                pl.ds(pl.multiple_of((i // 4) * 128, 128), 128),
            ]
            sent[rows, cols] = (
                value.astype(F32) * jnp.concatenate([lanes, lanes], axis=1)
            ).astype(BF16)

        z_copy(i).start()

        for step in range(NCH):
            if PASS_AT[step] or TAKE_AT[step]:
                @pl.when(i == step)
                def _():
                    for m in PASS_AT[step]:
                        pass_on(m)
                    for m in TAKE_AT[step]:
                        take_in(m)

        @pl.when(i >= LAG)
        def _():
            add_matched(i - LAG)

    for m in AFTER_PASS:
        pass_on(m)
    for m in AFTER_TAKE:
        take_in(m)
    for m in range(4 * NSUB):
        cross(m)

    @pl.loop(0, NCH)
    def _(step):
        u = step // 2
        half = lax.rem(step + core, 2)
        rows = pl.ds(pl.multiple_of((half * (NCH // 2) + u) * CH, CH), CH)

        @pl.when(half != core)
        def _():
            for n in range(NSUB):
                core_arrival(u, n).wait_recv()

        @pl.loop(0, HALF // 512)
        def _(n):
            cols = pl.ds(pl.multiple_of(n * 512, 512), 512)
            acc[rows, cols] += jnp.dot(bt[rows, :], mixed[:, cols], preferred_element_type=F32)

    for i in range(NCH - LAG, NCH - 1):
        add_matched(i)
    z_copy(NCH - 1).wait_recv()

    loads[1].wait()
    offset = col * HALF - row * NB

    def out_copy(t):
        rows = pl.ds(pl.multiple_of(t * CH, CH), CH)
        return pltpu.make_async_copy(sent.at[rows], new_sim.at[rows], out_sem.at[t])

    def line_of(t):
        return pl.ds(pl.multiple_of(t * 128, 128), 128)

    def give_copy(t):
        rows = pl.ds(pl.multiple_of(t * CH + (1 - core) * 128, 128), 128)
        return remote(
            acc.at[rows, pl.ds(0, F)], inv_scale.at[line_of(t)], sp.at[t], rp.at[t], sibling
        )

    def part_copy(t):
        device = (row, 2 * t + core)
        return remote(part.at[line_of(t)], slots.at[block], sa.at[t], ra.at[block], device)

    def part_arrival(i):
        return remote(part.at[line_of(0)], slots.at[i], sa.at[i], ra.at[i], sibling)

    def settle(t):
        give_copy(t).wait_recv()
        rows = pl.ds(pl.multiple_of(t * CH + core * 128, 128), 128)
        kept = acc[rows, pl.ds(0, F)] + inv_scale[line_of(t), :]

        @pl.when(t != block)
        def _():
            part[line_of(t), :] = kept.astype(BF16)
            part_copy(t).start()

        @pl.when(t == block)
        def _():
            total[...] = kept

    @pl.loop(0, NCH)
    def _(i):
        z_copy(i).wait_send()

    @pl.loop(0, NCH)
    def _(step):
        t = (step + block + 1) % NCH
        rows = pl.ds(pl.multiple_of(t * CH, CH), CH)
        value = decay_factor * (acc[rows, :] + gathered(rows, NCH - 1))
        down = lax.broadcasted_iota(jnp.int32, (CH, HALF), 0) + t * CH
        across = lax.broadcasted_iota(jnp.int32, (CH, HALF), 1) + offset
        value = jnp.where(down == across, 1.0, value).astype(BF16)
        sent[rows, :] = value
        out_copy(t).start()
        acc[rows, pl.ds(0, F)] = jnp.dot(value, feats[...], preferred_element_type=F32)
        give_copy(t).start()

        @pl.when(step > 0)
        def _():
            settle((step + block) % NCH)

    settle(block)

    @pl.loop(1, NCH)
    def _(i):
        source = (block + NCH - i) % NCH
        part_arrival(source).wait_recv()
        total[...] += slots[source].astype(F32)

    agg_copy = pltpu.make_async_copy(total, agg, agg_sem)
    agg_copy.start()

    @pl.loop(0, NCH)
    def _(i):
        x_copy(i).wait_send()
        own_copy(i).wait_send()
        forward(i).wait_send()
        out_copy(i).wait()

    for n in range(NSUB):
        for u in range(4):
            core_copy(u, n).wait_send()

            @pl.when(u != y)
            def _():
                along_y(u, n).wait_send()

        if n >= OVER_Z:
            over_z(2, n).wait_send()

            @pl.when(jnp.logical_not(home))
            def _():
                over_z(0, n).wait_send()

        for k in range(2):
            if k == 0 or n < OVER_Z:
                along_x(k, n, 0).wait_send()

                @pl.when(home)
                def _():
                    along_x(k, n, 1).wait_send()

    @pl.when(home)
    def _():
        near_half().wait_send()

    @pl.when(jnp.logical_not(home))
    def _():
        mirror_half().wait_send()

    @pl.loop(0, NCH)
    def _(t):
        give_copy(t).wait_send()

        @pl.when(t != block)
        def _():
            part_copy(t).wait_send()

    agg_copy.wait()


def finish(made, summed, new_sim, agg, held, held_sum, into, out):
    rows = [pl.ds(i * (NB // 4), NB // 4) for i in range(4)]
    reads = [pltpu.make_async_copy(made.at[r], held.at[r], into.at[i]) for i, r in enumerate(rows)]
    reads.append(pltpu.make_async_copy(summed, held_sum, into.at[4]))
    writes = [pltpu.make_async_copy(held.at[r], new_sim.at[r], out.at[i]) for i, r in enumerate(rows)]
    writes.append(pltpu.make_async_copy(held_sum, agg, out.at[4]))
    for read in reads:
        read.start()
    for read, write in zip(reads, writes):
        read.wait()
        write.start()
    for write in writes:
        write.wait()


def on_device(sim, diag_blocks, match_perm, match_scale, features):
    dma = pltpu.SemaphoreType.DMA
    made, summed, _ = pl.pallas_call(
        kernel,
        out_shape=(
            jax.ShapeDtypeStruct((NB, HALF), BF16),
            jax.ShapeDtypeStruct((128, F), F32),
            jax.ShapeDtypeStruct((4, PIECE, NB), BF16),
        ),
        in_specs=[
            pl.BlockSpec(memory_space=pl.ANY),
            pl.BlockSpec(memory_space=pl.ANY),
            pl.BlockSpec(memory_space=pltpu.VMEM),
            pl.BlockSpec(memory_space=pltpu.VMEM),
            pl.BlockSpec(memory_space=pl.ANY),
        ],
        out_specs=(
            pl.BlockSpec(memory_space=pl.ANY),
            pl.BlockSpec(memory_space=pl.ANY),
            pl.BlockSpec(memory_space=pl.ANY),
        ),
        scratch_shapes=[
            pltpu.VMEM((2, NB, HALF), BF16),
            pltpu.VMEM((2, NB, HALF), BF16),
            pltpu.VMEM((NB, HALF), BF16),
            pltpu.VMEM((NB, HALF), BF16),
            pltpu.VMEM((NB, HALF), BF16),
            pltpu.VMEM((NB, HALF), BF16),
            pltpu.VMEM((NB, HALF), BF16),
            pltpu.VMEM((NB, NB), BF16),
            pltpu.VMEM((NB, HALF), F32),
            pltpu.VMEM((HALF, F), BF16),
            pltpu.VMEM((PIECE, NB), BF16),
            pltpu.VMEM((8, NB), jnp.int32),
            pltpu.VMEM((8, NB), F32),
            pltpu.VMEM((NB, 128), jnp.int32),
            pltpu.VMEM((HALF, 256), F32),
            pltpu.VMEM((HALF, F), BF16),
            pltpu.VMEM((8, 128, F), BF16),
            pltpu.VMEM((128, F), F32),
            dma((2,)), dma((NCH,)),
            dma((NCH,)), dma((NCH,)),
            dma((NCH,)), dma((NCH,)),
            dma((NCH,)), dma((NCH,)),
            dma((NCH,)), dma((NCH,)),
            dma((2,)), dma((2,)),
            dma((2, 2, NSUB)), dma((4, NSUB)), dma((2, NSUB)),
            dma((4, NSUB)), dma((4, NSUB)),
            dma((4, NSUB)), dma((4, NSUB)),
            dma((8,)), dma((8,)),
            dma((8,)), dma((8,)),
            dma((NCH,)), dma(()),
        ],
        compiler_params=pltpu.CompilerParams(
            collective_id=0, has_side_effects=True, vmem_limit_bytes=60 * 2**20
        ),
        name="simrank",
    )(sim, diag_blocks, match_perm, match_scale, features)
    hbm = pl.BlockSpec(memory_space=pl.ANY)
    return pl.pallas_call(
        finish,
        out_shape=(
            jax.ShapeDtypeStruct((NB, HALF), BF16),
            jax.ShapeDtypeStruct((128, F), F32),
        ),
        in_specs=[hbm, hbm],
        out_specs=(hbm, hbm),
        scratch_shapes=[
            pltpu.VMEM((NB, HALF), BF16),
            pltpu.VMEM((128, F), F32),
            dma((5,)),
            dma((5,)),
        ],
        name="finish",
    )(made, summed)


def solution(mesh):
    placed = (P("row", "col"), P(None, "col"), P(), P(), P("col", None))
    return jax.shard_map(
        on_device,
        mesh=mesh,
        in_specs=placed,
        out_specs=(P("row", "col"), P(("row", "col"), None)),
        check_vma=False,
    )
```

```python
import jax
import jax.numpy as jnp
from jax import lax
from jax.experimental import pallas as pl
from jax.experimental.pallas import tpu as pltpu
from jax.sharding import PartitionSpec as P

decay_factor = 0.8
MESH = pl.DeviceIdType.MESH

NB = 2048
HALF = 1024
F = 256
CH = 256
NCH = NB // CH
PIECE = 256
NSUB = 4
OVER_Z = 2
SUB = PIECE // NSUB
AHEAD = 2
LAG = 2
PASS_AT = ((0, 1, 2, 3), (4, 5, 6, 7), (), (), (), (), (), ())
TAKE_AT = ((), (0, 1, 2, 3), (4, 5, 6, 7), (), (), (), (), ())
AFTER_PASS = ()
AFTER_TAKE = ()
BF16 = jnp.bfloat16
F32 = jnp.float32


def kernel(
    sim, diag, perm, scale, feat,
    new_sim, agg, relay,
    s_own, s_par, b_own, onehot, mixed, sent, marr, bt, acc, feats,
    mine_t, perm_row, scale_row, perm_col, inv_scale, part, slots, total,
    load_sem, own_sem,
    sx, rx, sz, rz, sd, rd, sf, rf, sb, rb, sq, rq, sv, sy, ry, sc, rc, sp, rp, sa, ra, out_sem, agg_sem,
):
    row = lax.axis_index("row")
    col = lax.axis_index("col")
    zh, y = row // 4, row % 4
    x, zl, core = col // 4, (col // 2) % 2, col % 2
    block = col // 2
    sibling = (row, col + 1 - 2 * core)
    x_partner = (row, (col + 8) % 16)
    z_partner = ((row + 4) % 8, col)
    z_near = (row, col + 2 - 4 * zl)
    z_mirror = ((1 - zh) * 4 + y, x * 4 + (1 - zl) * 2 + core)
    x_pair = (row, col + 4 - 8 * (x % 2))
    x_other = (row, (col + 12 + 8 * (x % 2)) % 16)
    home = x // 2 == zh
    home_int = home.astype(jnp.int32)
    pair = 2 * lax.rem(x + 1 - home_int, 2)
    order = (pair + zl, pair + 1 - zl, 2 - pair + zl, 3 - pair - zl)
    held = 2 * (x % 2) + zl

    barrier = pltpu.get_barrier_semaphore()

    def greet(device):
        pl.semaphore_signal(barrier, inc=1, device_id=device, device_id_type=MESH)

    for i in range(1, 16):
        greet((row, (col + i) % 16))
    for i in range(1, 4):
        greet((zh * 4 + (y + i) % 4, col))
    greet(z_partner)
    greet(z_mirror)

    loads = [
        pltpu.make_async_copy(diag, b_own, load_sem.at[0]),
        pltpu.make_async_copy(feat, feats, load_sem.at[1]),
    ]
    for load in loads:
        load.start()

    def own_load(i):
        rows = pl.ds(i * CH, CH)
        return pltpu.make_async_copy(
            sim.at[rows], s_own.at[core, rows], own_sem.at[i]
        )

    for i in range(NCH):
        own_load(i).start()
    pl.semaphore_wait(barrier, 20)

    def remote(src, dst, send, recv, device):
        return pltpu.make_async_remote_copy(
            src_ref=src, dst_ref=dst, send_sem=send, recv_sem=recv,
            device_id=device, device_id_type=MESH,
        )

    def x_copy(i):
        rows = pl.ds(i * CH, CH)
        return remote(sim.at[rows], s_par.at[core, rows], sx.at[i], rx.at[i], x_partner)

    def own_copy(i):
        rows = pl.ds(i * CH, CH)
        return remote(sim.at[rows], s_own.at[core, rows], sd.at[i], rd.at[i], sibling)

    def own_arrival(i):
        rows = pl.ds(i * CH, CH)
        return remote(sim.at[rows], s_own.at[1 - core, rows], sd.at[i], rd.at[i], sibling)

    def forward(i):
        rows = pl.ds(i * CH, CH)
        return remote(s_par.at[core, rows], s_par.at[core, rows], sf.at[i], rf.at[i], sibling)

    def forward_arrival(i):
        rows = pl.ds(i * CH, CH)
        return remote(s_par.at[core, rows], s_par.at[1 - core, rows], sf.at[i], rf.at[i], sibling)

    def z_copy(i):
        rows = pl.ds(i * CH, CH)
        return remote(sent.at[rows], marr.at[rows], sz.at[i], rz.at[i], z_partner)

    def bt_rows(half, part_of):
        return bt.at[pl.ds(pl.multiple_of(half * HALF + part_of * PIECE, PIECE), PIECE)]

    def near_half():
        rows = pl.ds(0, PIECE // 2)
        return remote(
            mine_t.at[rows], relay.at[held, rows], sb.at[0], rb.at[0], z_near
        )

    def mirror_half():
        rows = pl.ds(PIECE // 2, PIECE // 2)
        return remote(
            mine_t.at[rows], relay.at[held, rows], sb.at[1], rb.at[1], z_mirror
        )

    def held_copy(n):
        rows = pl.ds(n * SUB, SUB)
        return pltpu.make_async_copy(mine_t.at[rows], relay.at[held, rows], rq.at[held, n])

    def sub(n):
        return pl.ds(n * SUB, SUB)

    def along_x(k, n, where):
        device = (x_pair, x_other)[where]
        source = order[k]
        return remote(
            relay.at[source, sub(n)], relay.at[source, sub(n)],
            sq.at[k % 2, where, n], rq.at[source, n], device,
        )

    def bt_sub(half, u, n):
        start = pl.multiple_of(half * HALF + u * PIECE + n * SUB, SUB)
        return bt.at[pl.ds(start, SUB)]

    def along_y(target, n):
        return remote(
            relay.at[target, sub(n)], bt_sub(core, y, n),
            sy.at[target, n], ry.at[y, n], (zh * 4 + target, col),
        )

    def stay(n):
        return pltpu.make_async_copy(relay.at[y, sub(n)], bt_sub(core, y, n), ry.at[y, n])

    def y_arrival(u, n):
        return remote(mine_t.at[sub(n)], bt_sub(core, u, n), sy.at[u, n], ry.at[u, n], sibling)

    def core_copy(u, n):
        return remote(
            bt_sub(core, u, n), bt_sub(core, u, n), sc.at[u, n], rc.at[u, n], sibling
        )

    def core_arrival(u, n):
        return remote(
            mine_t.at[sub(n)], bt_sub(1 - core, u, n), sc.at[u, n], rc.at[u, n], sibling
        )

    def give_y(target, n):
        @pl.when(target != y)
        def _():
            along_y(target, n).start()

        @pl.when(target == y)
        def _():
            stay(n).start()

    def over_z(k, n):
        source = order[k]
        return remote(
            relay.at[source, sub(n)], relay.at[source, sub(n)],
            sv.at[k // 2, n], rq.at[source, n], z_near,
        )

    def hand_out(k):
        for n in range(NSUB if k == 0 else OVER_Z):
            along_x(k, n, 1).start()
        for n in range(NSUB if k == 0 else OVER_Z):
            along_x(k, n, 0).start()
        for n in range(NSUB):
            give_y(order[k], n)

    def pass_on(m):
        k, n = m // NSUB, m % NSUB

        @pl.when(jnp.logical_not(home))
        def _():
            along_x(k, n, 0).wait_recv()
            if k == 0 or n < OVER_Z:
                along_x(k, n, 0).start()
            if k == 0 and n >= OVER_Z:
                over_z(k, n).start()
            give_y(order[k], n)

    def take_in(m):
        k, n = 2 + m // NSUB, m % NSUB
        along_x(k, n, 0).wait_recv()
        if k == 2 and n >= OVER_Z:
            over_z(k, n).start()
        give_y(order[k], n)

    def cross(m):
        u, n = m // NSUB, m % NSUB
        y_arrival(u, n).wait_recv()
        core_copy(u, n).start()

    for i in range(AHEAD):
        x_copy(i).start()
    for i in range(NCH):
        own_copy(i).start()

    loads[0].wait()
    piece_cols = pl.ds(pl.multiple_of(y * PIECE, PIECE), PIECE)
    for i in range(NB // PIECE):
        rows = pl.ds(i * PIECE, PIECE)
        mine_t[:, rows] = b_own[rows, piece_cols].astype(F32).T.astype(BF16)

    @pl.when(home)
    def _():
        near_half().start()
        for n in range(NSUB):
            held_copy(n).start()
        for n in range(NSUB):
            held_copy(n).wait()
        hand_out(0)

    @pl.when(jnp.logical_not(home))
    def _():
        mirror_half().start()

    col_source = (block + 4) % 8
    row_source = (row + 4) % 8
    lines = lax.broadcasted_iota(jnp.int32, (8, NB), 0)

    def line(table, wanted):
        return jnp.sum(jnp.where(lines == wanted, table[...], 0), axis=0, keepdims=True)

    perm_row[0:1, :] = line(perm, col_source)
    perm_row[1:2, :] = line(perm, row_source)
    perm_row[2:3, :] = line(perm, row)
    scale_row[0:1, :] = line(scale, col_source)
    scale_row[1:2, :] = line(scale, row)

    half_cols = pl.ds(pl.multiple_of(core * HALF, HALF), HALF)

    @pl.loop(0, NB // 128)
    def _(i):
        rows = pl.ds(i * 128, 128)
        wanted = perm_row[0:1, half_cols]
        here = lax.broadcasted_iota(jnp.int32, (128, HALF), 0) + i * 128
        onehot[rows, :] = jnp.where(here == wanted, 1.0, 0.0).astype(BF16)

    for i in range(NB // 128):
        part_row = perm_row[1:2, pl.ds(i * 128, 128)]
        perm_col[pl.ds(i * 128, 128), :] = jnp.broadcast_to(part_row, (128, 128)).T

    @pl.loop(0, NB // 128)
    def _(i):
        here = lax.broadcasted_iota(jnp.int32, (128, NB), 0) + i * 128
        hit = jnp.where(here == perm_row[2:3, :], scale_row[1:2, :], 0.0)
        place = pl.ds(pl.multiple_of((i % 8) * 128, 128), 128)
        lanes = pl.ds(pl.multiple_of((i // 8) * 128, 128), 128)
        inv_scale[place, lanes] = jnp.broadcast_to(
            jnp.sum(hit, axis=1, keepdims=True), (128, 128)
        )

    def gathered(rows, i):
        wanted = perm_col[rows, :]
        wanted = jnp.concatenate([wanted, wanted], axis=1)
        here = lax.broadcasted_iota(jnp.int32, (CH, CH), 1) + i * CH
        pick = jnp.where(here == wanted, 1.0, 0.0).astype(BF16)
        far = marr[pl.ds(pl.multiple_of(i * CH, CH), CH), :]
        return jnp.dot(pick, far, preferred_element_type=F32)

    def add_matched(i):
        z_copy(i).wait_recv()

        @pl.loop(0, NCH)
        def _(t):
            rows = pl.ds(pl.multiple_of(t * CH, CH), CH)
            far = gathered(rows, i)

            @pl.when(i == 0)
            def _():
                acc[rows, :] = far

            @pl.when(i > 0)
            def _():
                acc[rows, :] += far

    @pl.when(home)
    def _():
        near_half().wait_recv()
        mirror_half().wait_recv()
        hand_out(1)

    @pl.loop(0, NCH)
    def _(i):
        rows = pl.ds(pl.multiple_of(i * CH, CH), CH)

        @pl.when(i + AHEAD < NCH)
        def _():
            x_copy(i + AHEAD).start()

        x_copy(i).wait_recv()
        forward(i).start()

        own_load(i).wait()
        own_arrival(i).wait_recv()
        forward_arrival(i).wait_recv()

        @pl.loop(0, HALF // 256)
        def _(n):
            cols = pl.ds(pl.multiple_of(n * 256, 256), 256)
            value = jnp.dot(s_own[0, rows, :], b_own[:HALF, cols], preferred_element_type=F32)
            value += jnp.dot(s_own[1, rows, :], b_own[HALF:, cols], preferred_element_type=F32)
            moved = jnp.dot(s_par[0, rows, :], onehot[:HALF, cols], preferred_element_type=F32)
            moved += jnp.dot(s_par[1, rows, :], onehot[HALF:, cols], preferred_element_type=F32)
            here = pl.ds(pl.multiple_of(core * HALF + n * 256, 256), 256)
            value += moved * scale_row[0:1, here]
            value = value.astype(BF16)
            mixed[rows, cols] = value
            lanes = inv_scale[
                pl.ds(pl.multiple_of((i % 4) * CH, CH), CH),
                pl.ds(pl.multiple_of((i // 4) * 128, 128), 128),
            ]
            sent[rows, cols] = (
                value.astype(F32) * jnp.concatenate([lanes, lanes], axis=1)
            ).astype(BF16)

        z_copy(i).start()

        for step in range(NCH):
            if PASS_AT[step] or TAKE_AT[step]:
                @pl.when(i == step)
                def _():
                    for m in PASS_AT[step]:
                        pass_on(m)
                    for m in TAKE_AT[step]:
                        take_in(m)

        @pl.when(i >= LAG)
        def _():
            add_matched(i - LAG)

    for m in AFTER_PASS:
        pass_on(m)
    for m in AFTER_TAKE:
        take_in(m)
    for m in range(4 * NSUB):
        cross(m)

    @pl.loop(0, NCH)
    def _(step):
        u = step // 2
        half = lax.rem(step + core, 2)
        rows = pl.ds(pl.multiple_of((half * (NCH // 2) + u) * CH, CH), CH)

        @pl.when(half != core)
        def _():
            for n in range(NSUB):
                core_arrival(u, n).wait_recv()

        @pl.loop(0, HALF // 512)
        def _(n):
            cols = pl.ds(pl.multiple_of(n * 512, 512), 512)
            acc[rows, cols] += jnp.dot(bt[rows, :], mixed[:, cols], preferred_element_type=F32)

    for i in range(NCH - LAG, NCH - 1):
        add_matched(i)
    z_copy(NCH - 1).wait_recv()

    loads[1].wait()
    offset = col * HALF - row * NB

    def out_copy(t):
        rows = pl.ds(pl.multiple_of(t * CH, CH), CH)
        return pltpu.make_async_copy(sent.at[rows], new_sim.at[rows], out_sem.at[t])

    def line_of(t):
        return pl.ds(pl.multiple_of(t * 128, 128), 128)

    def give_copy(t):
        rows = pl.ds(pl.multiple_of(t * CH + (1 - core) * 128, 128), 128)
        return remote(
            acc.at[rows, pl.ds(0, F)], inv_scale.at[line_of(t)], sp.at[t], rp.at[t], sibling
        )

    def part_copy(t):
        device = (row, 2 * t + core)
        return remote(part.at[line_of(t)], slots.at[block], sa.at[t], ra.at[block], device)

    def part_arrival(i):
        return remote(part.at[line_of(0)], slots.at[i], sa.at[i], ra.at[i], sibling)

    def settle(t):
        give_copy(t).wait_recv()
        rows = pl.ds(pl.multiple_of(t * CH + core * 128, 128), 128)
        kept = acc[rows, pl.ds(0, F)] + inv_scale[line_of(t), :]

        @pl.when(t != block)
        def _():
            part[line_of(t), :] = kept.astype(BF16)
            part_copy(t).start()

        @pl.when(t == block)
        def _():
            total[...] = kept

    @pl.loop(0, NCH)
    def _(i):
        z_copy(i).wait_send()

    @pl.loop(0, NCH)
    def _(step):
        t = (step + block + 1) % NCH
        rows = pl.ds(pl.multiple_of(t * CH, CH), CH)
        value = decay_factor * (acc[rows, :] + gathered(rows, NCH - 1))
        down = lax.broadcasted_iota(jnp.int32, (CH, HALF), 0) + t * CH
        across = lax.broadcasted_iota(jnp.int32, (CH, HALF), 1) + offset
        value = jnp.where(down == across, 1.0, value).astype(BF16)
        sent[rows, :] = value
        out_copy(t).start()
        acc[rows, pl.ds(0, F)] = jnp.dot(value, feats[...], preferred_element_type=F32)
        give_copy(t).start()

        @pl.when(step > 0)
        def _():
            settle((step + block) % NCH)

    settle(block)

    @pl.loop(1, NCH)
    def _(i):
        source = (block + NCH - i) % NCH
        part_arrival(source).wait_recv()
        total[...] += slots[source].astype(F32)

    agg_copy = pltpu.make_async_copy(total, agg, agg_sem)
    agg_copy.start()

    @pl.loop(0, NCH)
    def _(i):
        x_copy(i).wait_send()
        own_copy(i).wait_send()
        forward(i).wait_send()
        out_copy(i).wait()

    for n in range(NSUB):
        for u in range(4):
            core_copy(u, n).wait_send()

            @pl.when(u != y)
            def _():
                along_y(u, n).wait_send()

        if n >= OVER_Z:
            over_z(2, n).wait_send()

            @pl.when(jnp.logical_not(home))
            def _():
                over_z(0, n).wait_send()

        for k in range(2):
            if k == 0 or n < OVER_Z:
                along_x(k, n, 0).wait_send()

                @pl.when(home)
                def _():
                    along_x(k, n, 1).wait_send()

    @pl.when(home)
    def _():
        near_half().wait_send()

    @pl.when(jnp.logical_not(home))
    def _():
        mirror_half().wait_send()

    @pl.loop(0, NCH)
    def _(t):
        give_copy(t).wait_send()

        @pl.when(t != block)
        def _():
            part_copy(t).wait_send()

    agg_copy.wait()


def finish(made, summed, new_sim, agg, held, held_sum, into, out):
    rows = [pl.ds(i * (NB // 4), NB // 4) for i in range(4)]
    reads = [pltpu.make_async_copy(made.at[r], held.at[r], into.at[i]) for i, r in enumerate(rows)]
    reads.append(pltpu.make_async_copy(summed, held_sum, into.at[4]))
    writes = [pltpu.make_async_copy(held.at[r], new_sim.at[r], out.at[i]) for i, r in enumerate(rows)]
    writes.append(pltpu.make_async_copy(held_sum, agg, out.at[4]))
    for read in reads:
        read.start()
    for read, write in zip(reads, writes):
        read.wait()
        write.start()
    for write in writes:
        write.wait()


def on_device(sim, diag_blocks, match_perm, match_scale, features):
    dma = pltpu.SemaphoreType.DMA
    made, summed, _ = pl.pallas_call(
        kernel,
        out_shape=(
            jax.ShapeDtypeStruct((NB, HALF), BF16),
            jax.ShapeDtypeStruct((128, F), F32),
            jax.ShapeDtypeStruct((4, PIECE, NB), BF16),
        ),
        in_specs=[
            pl.BlockSpec(memory_space=pl.ANY),
            pl.BlockSpec(memory_space=pl.ANY),
            pl.BlockSpec(memory_space=pltpu.VMEM),
            pl.BlockSpec(memory_space=pltpu.VMEM),
            pl.BlockSpec(memory_space=pl.ANY),
        ],
        out_specs=(
            pl.BlockSpec(memory_space=pl.ANY),
            pl.BlockSpec(memory_space=pl.ANY),
            pl.BlockSpec(memory_space=pl.ANY),
        ),
        scratch_shapes=[
            pltpu.VMEM((2, NB, HALF), BF16),
            pltpu.VMEM((2, NB, HALF), BF16),
            pltpu.VMEM((NB, HALF), BF16),
            pltpu.VMEM((NB, HALF), BF16),
            pltpu.VMEM((NB, HALF), BF16),
            pltpu.VMEM((NB, HALF), BF16),
            pltpu.VMEM((NB, HALF), BF16),
            pltpu.VMEM((NB, NB), BF16),
            pltpu.VMEM((NB, HALF), F32),
            pltpu.VMEM((HALF, F), BF16),
            pltpu.VMEM((PIECE, NB), BF16),
            pltpu.VMEM((8, NB), jnp.int32),
            pltpu.VMEM((8, NB), F32),
            pltpu.VMEM((NB, 128), jnp.int32),
            pltpu.VMEM((HALF, 256), F32),
            pltpu.VMEM((HALF, F), BF16),
            pltpu.VMEM((8, 128, F), BF16),
            pltpu.VMEM((128, F), F32),
            dma((2,)), dma((NCH,)),
            dma((NCH,)), dma((NCH,)),
            dma((NCH,)), dma((NCH,)),
            dma((NCH,)), dma((NCH,)),
            dma((NCH,)), dma((NCH,)),
            dma((2,)), dma((2,)),
            dma((2, 2, NSUB)), dma((4, NSUB)), dma((2, NSUB)),
            dma((4, NSUB)), dma((4, NSUB)),
            dma((4, NSUB)), dma((4, NSUB)),
            dma((8,)), dma((8,)),
            dma((8,)), dma((8,)),
            dma((NCH,)), dma(()),
        ],
        compiler_params=pltpu.CompilerParams(
            collective_id=0, has_side_effects=True, vmem_limit_bytes=60 * 2**20
        ),
        name="simrank",
    )(sim, diag_blocks, match_perm, match_scale, features)
    hbm = pl.BlockSpec(memory_space=pl.ANY)
    return pl.pallas_call(
        finish,
        out_shape=(
            jax.ShapeDtypeStruct((NB, HALF), BF16),
            jax.ShapeDtypeStruct((128, F), F32),
        ),
        in_specs=[hbm, hbm],
        out_specs=(hbm, hbm),
        scratch_shapes=[
            pltpu.VMEM((NB, HALF), BF16),
            pltpu.VMEM((128, F), F32),
            dma((5,)),
            dma((5,)),
        ],
        name="finish",
    )(made, summed)


def solution(mesh):
    placed = (P("row", "col"), P(None, "col"), P(), P(), P("col", None))
    return jax.shard_map(
        on_device,
        mesh=mesh,
        in_specs=placed,
        out_specs=(P("row", "col"), P(("row", "col"), None)),
        check_vma=False,
    )
```
